32 devices in a mesh: cell: 4 (over y, x), sub: 8 (over z, core).
Axes of the slice: x: 2, y: 2, z: 4, core: 2. Of those that a mesh axis runs over, the one named last changes fastest.
Arguments:
- shell_conc: float32 [4, 32, 10, 128, 128], P('cell', 'sub'), may hold values from 0.2 to 0.8
- heat_rise: float32 [4, 30, 128, 128], P('cell', None, 'sub'), may hold values from -5 to 5
- layer_current: float32 [4, 32, 128, 128], P('cell', 'sub'), may hold values from -4 to 4
- layer_counts: int32 [8], replicated, may hold values from 1 to 4, 30 in all
- contacts: int32 [4, 2], replicated, may hold values from -1 to 3, as said below
Outputs:
- conc_new: float32 [4, 32, 10, 128, 128], P('cell', 'sub')
- heat_new: float32 [4, 30, 128, 128], P('cell', None, 'sub')
The draws below stay inside these ranges and needn't reach their ends.
Inputs may be any that keep to these rules, and one draw needn't show every extreme that they name: `layer_counts`: entry d is the number of consecutive layers held by index d of sub, in order; the entries sum to 30 and the largest is exactly 4. `contacts`: row c names the cell below and the cell above cell c in one stacking order of all 4 cells, each cell once; -1 marks the two ends of the stack.
All inputs are finite; a program needn't handle non-finite values.
Results may differ from the reference program's by a relative error of at most 0.0003.
Values sent between devices are 32-bit elements; how exact they have to be, the bound alone decides.
A program may use at most 64 MiB of HBM per device.

```python
import math
import jax
import jax.numpy as jnp
import numpy as np
from jax import lax

LAYERS = 30
LSLOT = 4
SHELLS = 10
GX = 128
CELLS = 4
SUBS = 8
SLOTS = 32
GY = 128


def draw_contacts(key, part):
    stacking = jax.random.permutation(jax.random.fold_in(key, 11), CELLS).astype(jnp.int32)
    placing = jnp.zeros((CELLS,), jnp.int32).at[stacking].set(jnp.arange(CELLS, dtype=jnp.int32))
    padded = jnp.concatenate([jnp.full((1,), -1, jnp.int32), stacking, jnp.full((1,), -1, jnp.int32)])
    below_cell = padded[placing]
    above_cell = padded[placing + 2]
    return jnp.stack([below_cell, above_cell], axis=1).astype(jnp.int32)


def block_scale(stream_key, extent, shards, low, largest):
    factor_of = 1.0
    for dim, parts in shards:
        steps = jax.random.uniform(jax.random.fold_in(jax.random.fold_in(stream_key, 6), dim), (parts,), jnp.float32, low / len(shards), largest / len(shards))
        factor_of = factor_of * jnp.repeat(jnp.exp(steps), extent[dim] // parts).reshape((-1,) + (1,) * (len(extent) - 1 - dim))
    return factor_of


def length_profile(amount, total, bound, lean):
    weights = [(1 << 20) // math.isqrt(grade ** lean) + 1 for grade in range(2, amount + 1)]
    surplus, given = total - bound - (amount - 1), [1] * (amount - 1)
    while surplus > 0:
        candidates = [i for i in range(amount - 1) if given[i] < bound]
        pool, left = sum([weights[i] for i in candidates]), surplus
        for i in candidates:
            addition = min(bound - given[i], max(1, left * weights[i] // pool), surplus)
            given[i] = given[i] + addition
            surplus = surplus - addition
    return np.array([bound] + given)


def ragged_sizes(key, count, total, bound, slope):
    if count == 2:
        one = jax.random.randint(key, (), max(1, total - bound), min(bound, total - 1) + 1)
        return jnp.stack([one, total - one])
    lengths = jnp.asarray(length_profile(count, total, bound, slope), jnp.int32)
    twos = (count - 1) // 2
    source_of, sink = lengths[1:1 + 2 * twos:2], lengths[2:2 + 2 * twos:2]
    room = jnp.minimum(source_of - 1, bound - sink)
    moved = jax.random.randint(jax.random.fold_in(key, 1), (twos,), 0, 1 << 20) % (room + 1)
    lengths = lengths.at[1:1 + 2 * twos:2].set(source_of - moved).at[2:2 + 2 * twos:2].set(sink + moved)
    return lengths[jax.random.permutation(jax.random.fold_in(key, 2), count)]


def centred(stream_key, shape, scale, reach, cuts=(), kind=jnp.bfloat16):
    drawn = scale * jax.random.normal(stream_key, shape, jnp.float32)
    if cuts:
        drawn = drawn * block_scale(stream_key, shape, cuts, -0.22, 0.18)
    return jnp.clip(drawn, -reach, reach).astype(kind)


def setup_inputs(seed: int = 0) -> dict:
    key_of = jax.random.split(jax.random.key(seed), 6)
    return {
        "shell_conc": jnp.clip(0.2 + 0.6 * jax.random.uniform(key_of[0], (CELLS, SLOTS, SHELLS, GY, GX), jnp.float32) ** block_scale(key_of[0], (CELLS, SLOTS, SHELLS, GY, GX), ((0, 4), (1, 8)), -0.2, 0.2), 0.2, 0.8),
        "heat_rise": jnp.clip(jax.random.uniform(key_of[1], (CELLS, LAYERS, GY, GX), jnp.float32, -5.0, 5.0) * block_scale(key_of[1], (CELLS, LAYERS, GY, GX), ((0, 4), (2, 8)), -0.4, 0.0), -5.0, 5.0),
        "layer_current": centred(key_of[2], (CELLS, SLOTS, GY, GX), 1.0, 4.0, ((0, 4), (1, 8)), jnp.float32),
        "layer_counts": ragged_sizes(key_of[3], SUBS, LAYERS, LSLOT, 2).astype(jnp.int32),
        "contacts": draw_contacts(jax.random.fold_in(key_of[5], 71), 0),
    }


BASE_KELVIN = 298.15
RATE_ACTIVATION = 5000.0
DIFFUSION_ACTIVATION = 3000.0
RATE_CONSTANT = 0.5
VOLT_PER_KELVIN = 2.0 * 8.314462618 / 96485.33212
HEAT_SCALE = 10.0
ENTROPY_SLOPE = 0.001
DIFFUSION_STEP = 0.005
SURFACE_STEP = 0.005
INPLANE_CONDUCT = 0.25
THROUGH_CONDUCT = 2.0
CONTACT_CONDUCT = 0.5

def inverse_sine(value):
    magnitude = jnp.abs(value)
    rooted = jnp.sqrt(1.0 + magnitude * magnitude)
    positive = jnp.log1p(magnitude + magnitude * magnitude / (1.0 + rooted))
    return jnp.where(value < 0.0, -positive, positive)

def layer_tables(layer_counts, slot_count, layer_total):
    counts = layer_counts.astype(jnp.int32)
    finish = jnp.cumsum(counts).astype(jnp.int32)
    starts = (finish - counts).astype(jnp.int32)
    devices = counts.shape[0]
    device_ids = jnp.arange(devices, dtype=jnp.int32)
    slot_index = jnp.arange(devices * slot_count, dtype=jnp.int32)
    slot_owner = slot_index // slot_count
    slot_place = slot_index % slot_count
    owner_hits = slot_owner[:, None] == device_ids[None, :]
    owner_count = lax.optimization_barrier(jnp.sum(jnp.where(owner_hits, counts[None, :], 0), axis=1)).astype(jnp.int32)
    owner_start = lax.optimization_barrier(jnp.sum(jnp.where(owner_hits, starts[None, :], 0), axis=1)).astype(jnp.int32)
    live_slot = slot_place < owner_count
    slot_layer = jnp.minimum(owner_start + slot_place, layer_total - 1).astype(jnp.int32)
    layer_index = jnp.arange(layer_total, dtype=jnp.int32)
    layer_owner = lax.optimization_barrier(jnp.sum((finish[None, :] <= layer_index[:, None]).astype(jnp.int32), axis=1)).astype(jnp.int32)
    layer_hits = layer_owner[:, None] == device_ids[None, :]
    layer_start = lax.optimization_barrier(jnp.sum(jnp.where(layer_hits, starts[None, :], 0), axis=1)).astype(jnp.int32)
    layer_slot = (layer_owner * slot_count + layer_index - layer_start).astype(jnp.int32)
    return (live_slot, slot_layer, layer_slot)

def kinetics(surface, kelvin, current):
    reciprocal = 1.0 / BASE_KELVIN - 1.0 / kelvin
    base_rate = RATE_CONSTANT * jnp.exp(RATE_ACTIVATION * reciprocal) * jnp.sqrt(surface * (1.0 - surface))
    ratio_rate = current / (2.0 * base_rate)
    arcsine = inverse_sine(ratio_rate)
    overvoltage = VOLT_PER_KELVIN * kelvin * arcsine
    entropic = ENTROPY_SLOPE * (0.5 - surface)
    source = HEAT_SCALE * current * (overvoltage + kelvin * entropic)
    heat_slope = HEAT_SCALE * current * (VOLT_PER_KELVIN * arcsine - VOLT_PER_KELVIN * ratio_rate * RATE_ACTIVATION / (kelvin * jnp.sqrt(1.0 + ratio_rate * ratio_rate)) + entropic)
    return (source, heat_slope)

def particle(states, kelvin, current):
    shells = states.shape[1]
    speedup = jnp.exp(DIFFUSION_ACTIVATION * (1.0 / BASE_KELVIN - 1.0 / kelvin))
    volumes = [((radial + 1) ** 3 - radial ** 3) / (3.0 * shells ** 3) for radial in range(shells)]
    linkage = [DIFFUSION_STEP * speedup * ((radial + 1) ** 2 / shells ** 2 * shells) for radial in range(shells - 1)]
    uppers = []
    values = []
    for radial in range(shells):
        diagonal = volumes[radial] + jnp.zeros_like(kelvin)
        right_side = volumes[radial] * states[:, radial]
        if radial < shells - 1:
            diagonal = diagonal + linkage[radial]
        else:
            right_side = right_side - SURFACE_STEP * current
        if radial > 0:
            diagonal = diagonal + linkage[radial - 1] - linkage[radial - 1] * uppers[radial - 1]
            right_side = right_side + linkage[radial - 1] * values[radial - 1]
        if radial < shells - 1:
            uppers.append(linkage[radial] / diagonal)
        else:
            uppers.append(jnp.zeros_like(kelvin))
        values.append(right_side / diagonal)
    result = [None] * shells
    result[shells - 1] = values[shells - 1]
    for radial in range(shells - 2, -1, -1):
        result[radial] = values[radial] + uppers[radial] * result[radial + 1]
    return jnp.stack(result, axis=1)

def column_solve(right_side, heat_slope):
    layer_total = right_side.shape[1]
    uppers = []
    values = []
    for height in range(layer_total):
        diagonal = 1.0 - heat_slope[:, height]
        source = right_side[:, height]
        if height > 0:
            diagonal = diagonal + THROUGH_CONDUCT - THROUGH_CONDUCT * uppers[height - 1]
            source = source + THROUGH_CONDUCT * values[height - 1]
        if height < layer_total - 1:
            diagonal = diagonal + THROUGH_CONDUCT
        uppers.append(THROUGH_CONDUCT / diagonal)
        values.append(source / diagonal)
    result = [None] * layer_total
    result[layer_total - 1] = values[layer_total - 1]
    for height in range(layer_total - 2, -1, -1):
        result[height] = values[height] + uppers[height] * result[height + 1]
    return jnp.stack(result, axis=1)

def reference(shell_conc, heat_rise, layer_current, layer_counts, contacts):
    live_slot, slot_layer, layer_slot = layer_tables(layer_counts, LSLOT, LAYERS)
    slot_rise = jnp.take(heat_rise, slot_layer, axis=1)
    kelvin = BASE_KELVIN + slot_rise
    surface = shell_conc[:, :, SHELLS - 1]
    source, heat_slope = kinetics(surface, kelvin, layer_current)

    def per_cell(operands):
        return particle(operands[0], operands[1], operands[2])
    updated = lax.map(per_cell, (shell_conc, kelvin, layer_current))
    conc_new = jnp.where(live_slot[None, :, None, None, None], updated, 0.0)
    layer_source = jnp.take(source, layer_slot, axis=1)
    layer_slope = jnp.take(heat_slope, layer_slot, axis=1)
    lower_cell = contacts[:, 0]
    upper_cell = contacts[:, 1]
    below_face = jnp.where((lower_cell >= 0)[:, None, None], jnp.take(heat_rise[:, LAYERS - 1], jnp.maximum(lower_cell, 0), axis=0), 0.0)
    above_face = jnp.where((upper_cell >= 0)[:, None, None], jnp.take(heat_rise[:, 0], jnp.maximum(upper_cell, 0), axis=0), 0.0)
    padded = jnp.pad(heat_rise, ((0, 0), (0, 0), (1, 1), (1, 1)), mode='edge')
    laplace = padded[:, :, 2:, 1:-1] + padded[:, :, :-2, 1:-1] + padded[:, :, 1:-1, 2:] + padded[:, :, 1:-1, :-2] - 4.0 * heat_rise
    right_side = heat_rise + INPLANE_CONDUCT * laplace + layer_source - layer_slope * heat_rise
    first_row = right_side[:, 0] + CONTACT_CONDUCT * (below_face - heat_rise[:, 0])
    last_row = right_side[:, LAYERS - 1] + CONTACT_CONDUCT * (above_face - heat_rise[:, LAYERS - 1])
    right_side = jnp.concatenate([first_row[:, None], right_side[:, 1:LAYERS - 1], last_row[:, None]], axis=1)
    heat_new = column_solve(right_side, layer_slope)
    return (conc_new, heat_new)
```

```python
import functools

import jax
import jax.numpy as jnp
from jax import lax
from jax.experimental import pallas as pl
from jax.experimental.pallas import tpu as pltpu
from jax.sharding import PartitionSpec as P

BASE_KELVIN = 298.15
RATE_ACTIVATION = 5000.0
DIFFUSION_ACTIVATION = 3000.0
RATE_CONSTANT = 0.5
VOLT_PER_KELVIN = 2.0 * 8.314462618 / 96485.33212
HEAT_SCALE = 10.0
ENTROPY_SLOPE = 0.001
DIFFUSION_STEP = 0.005
SURFACE_STEP = 0.005
INPLANE_CONDUCT = 0.25
THROUGH_CONDUCT = 2.0
CONTACT_CONDUCT = 0.5
MESH = pl.DeviceIdType.MESH
GRANT = 24 << 20
PAIR = 2


def partner(me, offset):
    bit = 1
    result = me
    while bit <= offset:
        if offset & bit:
            result = result + bit * (1 - 2 * ((me // bit) % 2))
        bit *= 2
    return result


def inverse_sine(value):
    magnitude = jnp.abs(value)
    rooted = jnp.sqrt(1.0 + magnitude * magnitude)
    positive = jnp.log1p(magnitude + magnitude * magnitude / (1.0 + rooted))
    return jnp.where(value < 0.0, -positive, positive), rooted


def kinetics(surface, rise, current):
    kelvin = BASE_KELVIN + rise
    per_kelvin = 1.0 / kelvin
    reciprocal = rise * (1.0 / BASE_KELVIN) * per_kelvin
    ratio_rate = (
        current
        * jnp.exp(-RATE_ACTIVATION * reciprocal)
        * lax.rsqrt(surface * (1.0 - surface))
        * (0.5 / RATE_CONSTANT)
    )
    arcsine, rooted = inverse_sine(ratio_rate)
    entropic = ENTROPY_SLOPE * (0.5 - surface)
    scaled = HEAT_SCALE * current
    common = VOLT_PER_KELVIN * arcsine + entropic
    source = scaled * kelvin * common
    heat_slope = scaled * (
        common - (VOLT_PER_KELVIN * RATE_ACTIVATION) * ratio_rate * per_kelvin / rooted
    )
    return source, heat_slope


def kernel(
    cells, subs,
    counts_hbm, contacts_hbm, heat_hbm, conc, current,
    conc_in, right_side, pivots,
    heat, staged, slot_rise, current_in, surface_rows, current_rows,
    edges, low_edge, high_edge, faces, base, extra, diagonal, layer_slot, counts, contacts,
    reach, cell_reach, own_sem, heat_send, heat_recv, surf_send, surf_recv, curr_send, curr_recv,
    edge_send, edge_recv, face_send, face_recv,
):
    cell = lax.axis_index("cell")
    sub = lax.axis_index("sub")
    slots, shells, gy, gx = conc_in.shape
    layers, rows, _ = heat.shape[1:]

    offsets = list(range(1, subs))
    arrivals = offsets[: PAIR - 1] + offsets[2 * PAIR - 2 : PAIR - 2 : -1] + offsets[: 2 * PAIR - 2 : -1]
    chip, core, chips = sub // PAIR, sub % PAIR, subs // PAIR
    cell_bits = [1 << bit for bit in range(cells.bit_length() - 1)]

    def has_chip(shift):
        return jnp.logical_and(chip + shift >= 0, chip + shift < chips)

    def on_chip(shift, place):
        return jnp.clip(chip + shift, 0, chips - 1) * PAIR + place

    def at_sub(index):
        return (cell, index)

    first_loads = [
        pltpu.make_async_copy(counts_hbm, counts, own_sem.at[5]),
        pltpu.make_async_copy(heat_hbm, heat, own_sem.at[4]),
        pltpu.make_async_copy(contacts_hbm, contacts, own_sem.at[6]),
    ]
    for load in first_loads:
        load.start()
    barrier = pltpu.get_barrier_semaphore()

    def greet(device):
        pl.semaphore_signal(barrier, inc=1, device_id=device, device_id_type=MESH)

    for place in range(1, PAIR):
        greet(at_sub(chip * PAIR + (core + place) % PAIR))
    for shift in (-1, 1):

        @pl.when(has_chip(shift))
        def _():
            for place in range(PAIR):
                greet(at_sub(on_chip(shift, place)))

    for bit in cell_bits:
        greet((partner(cell, bit), sub))

    loads = [
        pltpu.make_async_copy(current.at[0], current_in, own_sem.at[0]),
        pltpu.make_async_copy(conc.at[0], conc_in, own_sem.at[1]),
    ]
    for load in loads:
        load.start()

    beside = has_chip(-1).astype(jnp.int32) + has_chip(1).astype(jnp.int32)
    pl.semaphore_wait(barrier, PAIR - 1 + PAIR * beside + len(cell_bits))

    def relay(distance):
        for way, shift in enumerate((1, -1)):

            @pl.when(jnp.logical_and(has_chip(-shift), has_chip(shift * (distance - 1))))
            def _():
                pl.semaphore_signal(
                    reach.at[way, distance - 1],
                    inc=1,
                    device_id=at_sub(on_chip(-shift, core)),
                    device_id_type=MESH,
                )

    def learn(distance):
        for way, shift in enumerate((1, -1)):

            @pl.when(has_chip(shift * distance))
            def _():
                pl.semaphore_wait(reach.at[way, distance - 1], 1)

    if chips > 2:
        relay(2)
    for stage, bit in enumerate(cell_bits[:-1]):
        pl.semaphore_signal(
            cell_reach.at[stage], inc=1, device_id=(partner(cell, bit), sub), device_id_type=MESH
        )
        if stage + 1 < len(cell_bits) - 1:
            pl.semaphore_wait(cell_reach.at[stage], 1)

    sends = []

    def rows_of(index):
        return pl.ds(pl.multiple_of(index * rows, rows), rows)

    def slots_of(index):
        return pl.ds(index * slots, slots)

    def heat_copy(source, target, device):
        return pltpu.make_async_remote_copy(
            src_ref=staged.at[slots_of(target)],
            dst_ref=slot_rise.at[:, rows_of(source)],
            send_sem=heat_send.at[target],
            recv_sem=heat_recv.at[source],
            device_id=at_sub(device),
            device_id_type=MESH,
        )

    def surf_copy(source, target, device):
        return pltpu.make_async_remote_copy(
            src_ref=conc.at[0, :, shells - 1, rows_of(target)],
            dst_ref=surface_rows.at[slots_of(source)],
            send_sem=surf_send.at[target],
            recv_sem=surf_recv.at[source],
            device_id=at_sub(device),
            device_id_type=MESH,
        )

    def curr_copy(source, target, device):
        return pltpu.make_async_remote_copy(
            src_ref=current.at[0, :, rows_of(target)],
            dst_ref=current_rows.at[slots_of(source)],
            send_sem=curr_send.at[target],
            recv_sem=curr_recv.at[source],
            device_id=at_sub(device),
            device_id_type=MESH,
        )

    inner = jnp.logical_and(has_chip(-1), has_chip(1))
    outer = jnp.logical_not(inner)

    def issue(distance, makers, when=True):
        for shift in (distance, -distance) if distance else (0,):

            @pl.when(jnp.logical_and(has_chip(shift), when))
            def _():
                for make in makers:
                    for place in range(PAIR) if distance else range(1, PAIR):
                        other = on_chip(shift, place if distance else (core + place) % PAIR)
                        make(sub, other, other).start()

    issue(1, (surf_copy, curr_copy), outer)
    for load in first_loads:
        load.wait()
    edges[0] = heat[0, :, 0]
    edges[1] = heat[0, :, rows - 1]
    start = jnp.int32(0)
    for index in range(subs):
        held = counts[index]
        for place in range(slots):
            layer = jnp.minimum(start + place, layers - 1)
            staged[index * slots + place] = heat[0, layer]
        start = start + held
    faces[cell] = jnp.zeros((2, rows, gx), jnp.float32)

    issue(1, (heat_copy,))
    issue(0, (heat_copy, surf_copy, curr_copy))
    to_below = pltpu.make_async_remote_copy(
        src_ref=edges.at[0],
        dst_ref=high_edge,
        send_sem=edge_send.at[0],
        recv_sem=edge_recv.at[0],
        device_id=at_sub(jnp.maximum(sub - 1, 0)),
        device_id_type=MESH,
    )
    to_above = pltpu.make_async_remote_copy(
        src_ref=edges.at[1],
        dst_ref=low_edge,
        send_sem=edge_send.at[1],
        recv_sem=edge_recv.at[1],
        device_id=at_sub(jnp.minimum(sub + 1, subs - 1)),
        device_id_type=MESH,
    )

    @pl.when(sub > 0)
    def _():
        to_below.start()

    @pl.when(sub < subs - 1)
    def _():
        to_above.start()

    far = range(chips - 1, 1, -1)
    for distance in range(2, chips):
        learn(distance)
        if distance + 1 < chips:
            relay(distance + 1)
    for distance in far:
        issue(distance, (heat_copy,))
    for distance in far:
        issue(distance, (surf_copy, curr_copy))

    issue(1, (surf_copy, curr_copy,), inner)

    def face_copies(source, device):
        return [
            pltpu.make_async_remote_copy(
                src_ref=heat_hbm.at[0, layer],
                dst_ref=faces.at[source, place],
                send_sem=face_send.at[2 * device + place],
                recv_sem=face_recv.at[2 * source + place],
                device_id=(device, sub),
                device_id_type=MESH,
            )
            for place, layer in ((0, 0), (1, layers - 1))
        ]

    if len(cell_bits) > 1:
        pl.semaphore_wait(cell_reach.at[len(cell_bits) - 2], 1)
    for offset in range(1, cells):
        for copy in face_copies(cell, partner(cell, offset)):
            copy.start()
            sends.append(copy)

    mine = [
        pltpu.make_async_copy(
            conc.at[0, :, shells - 1, rows_of(sub)], surface_rows.at[slots_of(sub)], own_sem.at[2]
        ),
        pltpu.make_async_copy(
            current.at[0, :, rows_of(sub)], current_rows.at[slots_of(sub)], own_sem.at[3]
        ),
    ]
    for copy in mine:
        copy.start()
    slot_rise[:, rows_of(sub)] = staged[slots_of(sub)]

    def slot_of(layer, carry):
        total = jnp.int32(0)
        slot = layer
        for index in range(subs):
            total = total + counts[index]
            slot = slot + jnp.where(total <= layer, slots - counts[index], 0)
        layer_slot[layer] = jnp.minimum(slot, subs * slots - 1)
        return carry

    lax.fori_loop(0, layers, slot_of, jnp.int32(0))

    live_count = counts[sub]
    live = lax.broadcasted_iota(jnp.int32, (slots, rows, gx), 0) < live_count
    volumes = [((r + 1) ** 3 - r**3) / (3.0 * shells**3) for r in range(shells)]
    weights = [DIFFUSION_STEP * ((r + 1) ** 2 / shells**2 * shells) for r in range(shells - 1)]

    def particle(where):
        rise = slot_rise[:, where]
        speedup = jnp.exp(
            (DIFFUSION_ACTIVATION / BASE_KELVIN) * rise / (BASE_KELVIN + rise)
        )
        uppers = []
        values = []
        link = None
        for r in range(shells):
            right = volumes[r] * conc_in[:, r, where]
            if r == shells - 1:
                right = right - SURFACE_STEP * current_in[:, where]
            pivot = volumes[r]
            if r > 0:
                pivot = pivot + link * (1.0 - uppers[r - 1])
                right = right + link * values[r - 1]
            if r < shells - 1:
                next_link = weights[r] * speedup
                pivot = pivot + next_link
            inverse = 1.0 / pivot
            if r < shells - 1:
                uppers.append(next_link * inverse)
                link = next_link
            values.append(right * inverse)
        result = values[shells - 1]
        conc_in[:, shells - 1, where] = jnp.where(live, result, 0.0)
        for r in range(shells - 2, -1, -1):
            result = values[r] + uppers[r] * result
            conc_in[:, r, where] = jnp.where(live, result, 0.0)

    for load in loads:
        load.wait()
    for offset in [0] + arrivals:
        other = partner(sub, offset)
        if offset:
            heat_copy(other, sub, other).wait_recv()
        particle(rows_of(other))

    @pl.when(sub > 0)
    def _():
        to_above.wait_recv()

    @pl.when(sub == 0)
    def _():
        low_edge[...] = edges[0]

    @pl.when(sub < subs - 1)
    def _():
        to_below.wait_recv()

    @pl.when(sub == subs - 1)
    def _():
        high_edge[...] = edges[1]

    for offset in range(1, cells):
        other = partner(cell, offset)
        for copy in face_copies(other, other):
            copy.wait_recv()

    row_index = lax.broadcasted_iota(jnp.int32, (rows, gx), 0)
    lane_index = lax.broadcasted_iota(jnp.int32, (rows, gx), 1)

    def fill(layer, carry):
        here = heat[0, layer]
        up = pltpu.roll(here, 1, 0)
        up = jnp.where(row_index == 0, low_edge[pl.ds(layer, 1)], up)
        down = pltpu.roll(here, rows - 1, 0)
        down = jnp.where(row_index == rows - 1, high_edge[pl.ds(layer, 1)], down)
        left = jnp.where(lane_index == 0, here, pltpu.roll(here, 1, 1))
        right = jnp.where(lane_index == gx - 1, here, pltpu.roll(here, gx - 1, 1))
        laplace = down + up + right + left - 4.0 * here
        base[layer] = here + INPLANE_CONDUCT * laplace
        return carry

    lax.fori_loop(0, layers, fill, jnp.int32(0), unroll=2)
    lower = contacts[0, cell]
    upper = contacts[1, cell]
    below_face = jnp.where(lower >= 0, faces[jnp.maximum(lower, 0), 1], 0.0)
    above_face = jnp.where(upper >= 0, faces[jnp.maximum(upper, 0), 0], 0.0)
    base[0] = base[0] + CONTACT_CONDUCT * (below_face - heat[0, 0])
    base[layers - 1] = base[layers - 1] + CONTACT_CONDUCT * (above_face - heat[0, layers - 1])

    for offset in [0] + arrivals:
        other = partner(sub, offset)
        if offset:
            surf_copy(other, sub, other).wait_recv()
            curr_copy(other, sub, other).wait_recv()
        else:
            for copy in mine:
                copy.wait()
        at = slots_of(other)
        rise = staged[at]
        source, slope = kinetics(surface_rows[at], rise, current_rows[at])
        extra[at] = source - slope * rise
        diagonal[at] = 1.0 - slope

    for layer in range(layers):
        slot = layer_slot[layer]
        ends = (layer > 0) + (layer < layers - 1)
        pivots[layer] = diagonal[slot] + ends * THROUGH_CONDUCT
        right_side[layer] = base[layer] + extra[slot]

    for offset in offsets:
        other = partner(sub, offset)
        for make in (heat_copy, surf_copy, curr_copy):
            make(sub, other, other).wait_send()
    for copy in sends:
        copy.wait_send()

    @pl.when(sub > 0)
    def _():
        to_below.wait_send()

    @pl.when(sub < subs - 1)
    def _():
        to_above.wait_send()


def finish(conc, right_side, pivots, conc_new, heat_out, heat_new, sem):
    slots = conc.shape[0]
    layers = right_side.shape[0]
    writes = [
        pltpu.make_async_copy(conc.at[s], conc_new.at[0, s], sem.at[s]) for s in range(slots)
    ]
    for write in writes:
        write.start()

    def sweep(order):
        factors, values = [], []
        for layer in order:
            pivot, right = pivots[layer], right_side[layer]
            if factors:
                pivot = pivot - THROUGH_CONDUCT * factors[-1]
                right = right + THROUGH_CONDUCT * values[-1]
            inverse = 1.0 / pivot
            factors.append(THROUGH_CONDUCT * inverse)
            values.append(right * inverse)
        return factors, values

    middle = layers // 2
    low_f, low_v = sweep(range(middle))
    high_f, high_v = sweep(range(layers - 1, middle - 1, -1))
    low = (low_v[-1] + low_f[-1] * high_v[-1]) / (1.0 - low_f[-1] * high_f[-1])
    high = high_v[-1] + high_f[-1] * low
    heat_new[0, middle - 1] = low
    heat_new[0, middle] = high
    for step in range(middle - 2, -1, -1):
        low = low_v[step] + low_f[step] * low
        heat_new[0, step] = low
    for step in range(len(high_v) - 2, -1, -1):
        high = high_v[step] + high_f[step] * high
        heat_new[0, layers - 1 - step] = high
    heat_write = pltpu.make_async_copy(heat_new, heat_out, sem.at[slots])
    heat_write.start()
    for write in writes:
        write.wait()
    heat_write.wait()


def per_device(cells, subs, shell_conc, heat_rise, layer_current, layer_counts, contacts):
    _, slots, shells, gy, gx = shell_conc.shape
    _, layers, rows, _ = heat_rise.shape
    f32 = jnp.float32
    dma = pltpu.SemaphoreType.DMA
    table = (layers, rows, gx)
    held = [
        pltpu.with_memory_space_constraint(array, pltpu.HBM)
        for array in (layer_counts, contacts.T, heat_rise, shell_conc, layer_current)
    ]
    conc, right_side, pivots = pl.pallas_call(
        functools.partial(kernel, cells, subs),
        out_shape=(
            pltpu.VMEM((slots, shells, gy, gx), f32),
            pltpu.VMEM(table, f32),
            pltpu.VMEM(table, f32),
        ),
        in_specs=[
            pl.BlockSpec(memory_space=pltpu.HBM)
        ] * 5,
        out_specs=(pl.BlockSpec(memory_space=pltpu.VMEM),) * 3,
        scratch_shapes=[
            pltpu.VMEM(heat_rise.shape, f32),
            pltpu.VMEM((subs * slots, rows, gx), f32),
            pltpu.VMEM((slots, gy, gx), f32),
            pltpu.VMEM((slots, gy, gx), f32),
            pltpu.VMEM((subs * slots, rows, gx), f32),
            pltpu.VMEM((subs * slots, rows, gx), f32),
            pltpu.VMEM((2, layers, gx), f32),
            pltpu.VMEM((layers, gx), f32),
            pltpu.VMEM((layers, gx), f32),
            pltpu.VMEM((cells, 2, rows, gx), f32),
            pltpu.VMEM(table, f32),
            pltpu.VMEM((subs * slots, rows, gx), f32),
            pltpu.VMEM((subs * slots, rows, gx), f32),
            pltpu.SMEM((layers,), jnp.int32),
            pltpu.SMEM(layer_counts.shape, jnp.int32),
            pltpu.SMEM(contacts.shape[::-1], jnp.int32),
            pltpu.SemaphoreType.REGULAR((2, max(subs // PAIR, 2))),
            pltpu.SemaphoreType.REGULAR((max(cells.bit_length() - 2, 1),)),
            dma((7,)),
            dma((subs,)),
            dma((subs,)),
            dma((subs,)),
            dma((subs,)),
            dma((subs,)),
            dma((subs,)),
            dma((2,)),
            dma((2,)),
            dma((2 * cells,)),
            dma((2 * cells,)),
        ],
        compiler_params=pltpu.CompilerParams(
            collective_id=0, has_side_effects=True, vmem_limit_bytes=GRANT
        ),
    )(*held)
    conc_new, heat_new = pl.pallas_call(
        finish,
        out_shape=(
            jax.ShapeDtypeStruct(shell_conc.shape, f32),
            jax.ShapeDtypeStruct(heat_rise.shape, f32),
        ),
        in_specs=[pl.BlockSpec(memory_space=pltpu.VMEM)] * 3,
        out_specs=(
            pl.BlockSpec(memory_space=pl.ANY),
            pl.BlockSpec(memory_space=pl.ANY),
        ),
        scratch_shapes=[pltpu.VMEM(heat_rise.shape, f32), dma((slots + 1,))],
        compiler_params=pltpu.CompilerParams(vmem_limit_bytes=GRANT),
    )(conc, right_side, pivots)
    return conc_new, heat_new


def solution(mesh):
    in_specs = (
        P("cell", "sub", None, None, None),
        P("cell", None, "sub", None),
        P("cell", "sub", None, None),
        P(),
        P(),
    )
    out_specs = (P("cell", "sub", None, None, None), P("cell", None, "sub", None))
    body = functools.partial(per_device, mesh.shape["cell"], mesh.shape["sub"])
    return jax.shard_map(
        body, mesh=mesh, in_specs=in_specs, out_specs=out_specs, check_vma=False
    )
```

```python
import functools

import jax
import jax.numpy as jnp
from jax import lax
from jax.experimental import pallas as pl
from jax.experimental.pallas import tpu as pltpu
from jax.sharding import PartitionSpec as P

BASE_KELVIN = 298.15
RATE_ACTIVATION = 5000.0
DIFFUSION_ACTIVATION = 3000.0
RATE_CONSTANT = 0.5
VOLT_PER_KELVIN = 2.0 * 8.314462618 / 96485.33212
HEAT_SCALE = 10.0
ENTROPY_SLOPE = 0.001
DIFFUSION_STEP = 0.005
SURFACE_STEP = 0.005
INPLANE_CONDUCT = 0.25
THROUGH_CONDUCT = 2.0
CONTACT_CONDUCT = 0.5
MESH = pl.DeviceIdType.MESH
GRANT = 24 << 20
PAIR = 2


def partner(me, offset):
    bit = 1
    result = me
    while bit <= offset:
        if offset & bit:
            result = result + bit * (1 - 2 * ((me // bit) % 2))
        bit *= 2
    return result


def inverse_sine(value):
    magnitude = jnp.abs(value)
    rooted = jnp.sqrt(1.0 + magnitude * magnitude)
    positive = jnp.log1p(magnitude + magnitude * magnitude / (1.0 + rooted))
    return jnp.where(value < 0.0, -positive, positive), rooted


def kinetics(surface, rise, current):
    kelvin = BASE_KELVIN + rise
    per_kelvin = 1.0 / kelvin
    reciprocal = rise * (1.0 / BASE_KELVIN) * per_kelvin
    ratio_rate = (
        current
        * jnp.exp(-RATE_ACTIVATION * reciprocal)
        * lax.rsqrt(surface * (1.0 - surface))
        * (0.5 / RATE_CONSTANT)
    )
    arcsine, rooted = inverse_sine(ratio_rate)
    entropic = ENTROPY_SLOPE * (0.5 - surface)
    scaled = HEAT_SCALE * current
    common = VOLT_PER_KELVIN * arcsine + entropic
    source = scaled * kelvin * common
    heat_slope = scaled * (
        common - (VOLT_PER_KELVIN * RATE_ACTIVATION) * ratio_rate * per_kelvin / rooted
    )
    return source, heat_slope


def kernel(
    cells, subs,
    counts_hbm, contacts_hbm, heat_hbm, conc, current,
    conc_in, right_side, pivots,
    heat, staged, slot_rise, current_in, surface_rows, current_rows,
    edges, low_edge, high_edge, faces, base, extra, diagonal, layer_slot, counts, contacts,
    reach, cell_reach, own_sem, heat_send, heat_recv, surf_send, surf_recv, curr_send, curr_recv,
    edge_send, edge_recv, face_send, face_recv,
):
    cell = lax.axis_index("cell")
    sub = lax.axis_index("sub")
    slots, shells, gy, gx = conc_in.shape
    layers, rows, _ = heat.shape[1:]

    offsets = list(range(1, subs))
    arrivals = offsets[: PAIR - 1] + offsets[2 * PAIR - 2 : PAIR - 2 : -1] + offsets[: 2 * PAIR - 2 : -1]
    chip, core, chips = sub // PAIR, sub % PAIR, subs // PAIR
    cell_bits = [1 << bit for bit in range(cells.bit_length() - 1)]

    def has_chip(shift):
        return jnp.logical_and(chip + shift >= 0, chip + shift < chips)

    def on_chip(shift, place):
        return jnp.clip(chip + shift, 0, chips - 1) * PAIR + place

    def at_sub(index):
        return (cell, index)

    first_loads = [
        pltpu.make_async_copy(counts_hbm, counts, own_sem.at[5]),
        pltpu.make_async_copy(heat_hbm, heat, own_sem.at[4]),
        pltpu.make_async_copy(contacts_hbm, contacts, own_sem.at[6]),
    ]
    for load in first_loads:
        load.start()
    barrier = pltpu.get_barrier_semaphore()

    def greet(device):
        pl.semaphore_signal(barrier, inc=1, device_id=device, device_id_type=MESH)

    for place in range(1, PAIR):
        greet(at_sub(chip * PAIR + (core + place) % PAIR))
    inward = jnp.where(2 * chip < chips, 1, -1)
    middle = jnp.logical_or(chip == chips // 2 - 1, chip == chips // 2)
    for shift in (-1, 1):

        @pl.when(jnp.logical_and(has_chip(shift), jnp.logical_or(inward != shift, middle)))
        def _():
            for place in range(PAIR):
                greet(at_sub(on_chip(shift, place)))

    for bit in cell_bits:

        @pl.when((cell // bit) % 2 == 0)
        def _():
            greet((partner(cell, bit), sub))

    loads = [
        pltpu.make_async_copy(current.at[0], current_in, own_sem.at[0]),
        pltpu.make_async_copy(conc.at[0], conc_in, own_sem.at[1]),
    ]
    for load in loads:
        load.start()

    lower = sum((cell // bit) % 2 for bit in cell_bits)
    pl.semaphore_wait(barrier, PAIR - 1 + (PAIR if chips > 1 else 0) + lower)

    def tell(semaphore, device):
        pl.semaphore_signal(semaphore, inc=1, device_id=device, device_id_type=MESH)

    for way, shift in enumerate((1, -1)):

        @pl.when(jnp.logical_and(inward == -shift, jnp.logical_not(middle)))
        def _():
            tell(reach.at[way, 0], at_sub(on_chip(-shift, core)))

    for place, bit in enumerate(cell_bits):

        @pl.when((cell // bit) % 2 == 1)
        def _():
            tell(cell_reach.at[0, place], (partner(cell, bit), sub))

    def relay(distance):
        for way, shift in enumerate((1, -1)):

            @pl.when(jnp.logical_and(has_chip(-shift), has_chip(shift * (distance - 1))))
            def _():
                tell(reach.at[way, distance - 1], at_sub(on_chip(-shift, core)))

    def learn(distance):
        for way, shift in enumerate((1, -1)):

            known = has_chip(shift * distance)
            if distance == 1:
                known = jnp.logical_and(known, inward != shift)

            @pl.when(known)
            def _():
                pl.semaphore_wait(reach.at[way, distance - 1], 1)

    sends = []

    def rows_of(index):
        return pl.ds(pl.multiple_of(index * rows, rows), rows)

    def slots_of(index):
        return pl.ds(index * slots, slots)

    def heat_copy(source, target, device):
        return pltpu.make_async_remote_copy(
            src_ref=staged.at[slots_of(target)],
            dst_ref=slot_rise.at[:, rows_of(source)],
            send_sem=heat_send.at[target],
            recv_sem=heat_recv.at[source],
            device_id=at_sub(device),
            device_id_type=MESH,
        )

    def surf_copy(source, target, device):
        return pltpu.make_async_remote_copy(
            src_ref=conc.at[0, :, shells - 1, rows_of(target)],
            dst_ref=surface_rows.at[slots_of(source)],
            send_sem=surf_send.at[target],
            recv_sem=surf_recv.at[source],
            device_id=at_sub(device),
            device_id_type=MESH,
        )

    def curr_copy(source, target, device):
        return pltpu.make_async_remote_copy(
            src_ref=current.at[0, :, rows_of(target)],
            dst_ref=current_rows.at[slots_of(source)],
            send_sem=curr_send.at[target],
            recv_sem=curr_recv.at[source],
            device_id=at_sub(device),
            device_id_type=MESH,
        )

    inner = jnp.logical_and(has_chip(-1), has_chip(1))
    outer = jnp.logical_not(inner)

    def issue(distance, makers, when=True, within=None):
        for shift in (distance, -distance) if distance else (0,):

            wanted = jnp.logical_and(has_chip(shift), when)
            if within is not None:
                wanted = jnp.logical_and(wanted, (inward == shift) == within)

            @pl.when(wanted)
            def _():
                for make in makers:
                    for place in range(PAIR) if distance else range(1, PAIR):
                        other = on_chip(shift, place if distance else (core + place) % PAIR)
                        make(sub, other, other).start()

    issue(1, (surf_copy, curr_copy), outer)
    for load in first_loads:
        load.wait()
    edges[0] = heat[0, :, 0]
    edges[1] = heat[0, :, rows - 1]
    start = jnp.int32(0)
    for index in range(subs):
        held = counts[index]
        for place in range(slots):
            layer = jnp.minimum(start + place, layers - 1)
            staged[index * slots + place] = heat[0, layer]
        start = start + held
    faces[cell] = jnp.zeros((2, rows, gx), jnp.float32)

    issue(1, (heat_copy,), within=True)
    learn(1)
    if chips > 2:
        relay(2)
    issue(1, (heat_copy,), within=False)
    issue(0, (heat_copy, surf_copy, curr_copy))
    to_below = pltpu.make_async_remote_copy(
        src_ref=edges.at[0],
        dst_ref=high_edge,
        send_sem=edge_send.at[0],
        recv_sem=edge_recv.at[0],
        device_id=at_sub(jnp.maximum(sub - 1, 0)),
        device_id_type=MESH,
    )
    to_above = pltpu.make_async_remote_copy(
        src_ref=edges.at[1],
        dst_ref=low_edge,
        send_sem=edge_send.at[1],
        recv_sem=edge_recv.at[1],
        device_id=at_sub(jnp.minimum(sub + 1, subs - 1)),
        device_id_type=MESH,
    )

    @pl.when(sub > 0)
    def _():
        to_below.start()

    @pl.when(sub < subs - 1)
    def _():
        to_above.start()

    far = range(chips - 1, 1, -1)
    for distance in range(2, chips):
        learn(distance)
        if distance + 1 < chips:
            relay(distance + 1)
    for distance in far:
        issue(distance, (heat_copy, surf_copy, curr_copy))

    def face_copies(source, device):
        return [
            pltpu.make_async_remote_copy(
                src_ref=heat_hbm.at[0, layer],
                dst_ref=faces.at[source, place],
                send_sem=face_send.at[2 * device + place],
                recv_sem=face_recv.at[2 * source + place],
                device_id=(device, sub),
                device_id_type=MESH,
            )
            for place, layer in ((0, 0), (1, layers - 1))
        ]

    for place, bit in enumerate(cell_bits):

        @pl.when((cell // bit) % 2 == 0)
        def _():
            pl.semaphore_wait(cell_reach.at[0, place], 1)

    def spread(place):
        tell(cell_reach.at[1, place], (partner(cell, cell_bits[place]), sub))

    if len(cell_bits) > 1:
        spread(0)

    def send_faces():
        for place in range(len(cell_bits) - 1):
            pl.semaphore_wait(cell_reach.at[1, place], 1)
            if place + 1 < len(cell_bits) - 1:
                spread(place + 1)
        for offset in range(1, cells):
            for copy in face_copies(cell, partner(cell, offset)):
                copy.start()
                sends.append(copy)


    mine = [
        pltpu.make_async_copy(
            conc.at[0, :, shells - 1, rows_of(sub)], surface_rows.at[slots_of(sub)], own_sem.at[2]
        ),
        pltpu.make_async_copy(
            current.at[0, :, rows_of(sub)], current_rows.at[slots_of(sub)], own_sem.at[3]
        ),
    ]
    for copy in mine:
        copy.start()
    slot_rise[:, rows_of(sub)] = staged[slots_of(sub)]

    def slot_of(layer, carry):
        total = jnp.int32(0)
        slot = layer
        for index in range(subs):
            total = total + counts[index]
            slot = slot + jnp.where(total <= layer, slots - counts[index], 0)
        layer_slot[layer] = jnp.minimum(slot, subs * slots - 1)
        return carry

    lax.fori_loop(0, layers, slot_of, jnp.int32(0))

    live_count = counts[sub]
    live = lax.broadcasted_iota(jnp.int32, (slots, rows, gx), 0) < live_count
    volumes = [((r + 1) ** 3 - r**3) / (3.0 * shells**3) for r in range(shells)]
    weights = [DIFFUSION_STEP * ((r + 1) ** 2 / shells**2 * shells) for r in range(shells - 1)]

    def particle(where):
        rise = slot_rise[:, where]
        speedup = jnp.exp(
            (DIFFUSION_ACTIVATION / BASE_KELVIN) * rise / (BASE_KELVIN + rise)
        )
        uppers = []
        values = []
        link = None
        for r in range(shells):
            right = volumes[r] * conc_in[:, r, where]
            if r == shells - 1:
                right = right - SURFACE_STEP * current_in[:, where]
            pivot = volumes[r]
            if r > 0:
                pivot = pivot + link * (1.0 - uppers[r - 1])
                right = right + link * values[r - 1]
            if r < shells - 1:
                next_link = weights[r] * speedup
                pivot = pivot + next_link
            inverse = 1.0 / pivot
            if r < shells - 1:
                uppers.append(next_link * inverse)
                link = next_link
            values.append(right * inverse)
        result = values[shells - 1]
        conc_in[:, shells - 1, where] = jnp.where(live, result, 0.0)
        for r in range(shells - 2, -1, -1):
            result = values[r] + uppers[r] * result
            conc_in[:, r, where] = jnp.where(live, result, 0.0)

    for load in loads:
        load.wait()
    for count, offset in enumerate([0] + arrivals):
        other = partner(sub, offset)
        if offset:
            heat_copy(other, sub, other).wait_recv()
        if count == 4:
            issue(1, (surf_copy, curr_copy), inner, True)
        if count == 2:
            issue(1, (surf_copy, curr_copy), inner, False)
        particle(rows_of(other))
        if count == 0:
            send_faces()

    @pl.when(sub > 0)
    def _():
        to_above.wait_recv()

    @pl.when(sub == 0)
    def _():
        low_edge[...] = edges[0]

    @pl.when(sub < subs - 1)
    def _():
        to_below.wait_recv()

    @pl.when(sub == subs - 1)
    def _():
        high_edge[...] = edges[1]

    for offset in range(1, cells):
        other = partner(cell, offset)
        for copy in face_copies(other, other):
            copy.wait_recv()

    row_index = lax.broadcasted_iota(jnp.int32, (rows, gx), 0)
    lane_index = lax.broadcasted_iota(jnp.int32, (rows, gx), 1)

    def fill(layer, carry):
        here = heat[0, layer]
        up = pltpu.roll(here, 1, 0)
        up = jnp.where(row_index == 0, low_edge[pl.ds(layer, 1)], up)
        down = pltpu.roll(here, rows - 1, 0)
        down = jnp.where(row_index == rows - 1, high_edge[pl.ds(layer, 1)], down)
        left = jnp.where(lane_index == 0, here, pltpu.roll(here, 1, 1))
        right = jnp.where(lane_index == gx - 1, here, pltpu.roll(here, gx - 1, 1))
        laplace = down + up + right + left - 4.0 * here
        base[layer] = here + INPLANE_CONDUCT * laplace
        return carry

    lax.fori_loop(0, layers, fill, jnp.int32(0), unroll=2)
    lower = contacts[0, cell]
    upper = contacts[1, cell]
    below_face = jnp.where(lower >= 0, faces[jnp.maximum(lower, 0), 1], 0.0)
    above_face = jnp.where(upper >= 0, faces[jnp.maximum(upper, 0), 0], 0.0)
    base[0] = base[0] + CONTACT_CONDUCT * (below_face - heat[0, 0])
    base[layers - 1] = base[layers - 1] + CONTACT_CONDUCT * (above_face - heat[0, layers - 1])

    for offset in [0] + arrivals:
        other = partner(sub, offset)
        if offset:
            surf_copy(other, sub, other).wait_recv()
            curr_copy(other, sub, other).wait_recv()
        else:
            for copy in mine:
                copy.wait()
        at = slots_of(other)
        rise = staged[at]
        source, slope = kinetics(surface_rows[at], rise, current_rows[at])
        extra[at] = source - slope * rise
        diagonal[at] = 1.0 - slope

    for layer in range(layers):
        slot = layer_slot[layer]
        ends = (layer > 0) + (layer < layers - 1)
        pivots[layer] = diagonal[slot] + ends * THROUGH_CONDUCT
        right_side[layer] = base[layer] + extra[slot]

    for offset in offsets:
        other = partner(sub, offset)
        for make in (heat_copy, surf_copy, curr_copy):
            make(sub, other, other).wait_send()
    for copy in sends:
        copy.wait_send()

    @pl.when(sub > 0)
    def _():
        to_below.wait_send()

    @pl.when(sub < subs - 1)
    def _():
        to_above.wait_send()


def finish(conc, right_side, pivots, conc_new, heat_out, heat_new, sem):
    slots = conc.shape[0]
    layers = right_side.shape[0]
    writes = [
        pltpu.make_async_copy(conc.at[s], conc_new.at[0, s], sem.at[s]) for s in range(slots)
    ]
    for write in writes:
        write.start()

    def sweep(order):
        factors, values = [], []
        for layer in order:
            pivot, right = pivots[layer], right_side[layer]
            if factors:
                pivot = pivot - THROUGH_CONDUCT * factors[-1]
                right = right + THROUGH_CONDUCT * values[-1]
            inverse = 1.0 / pivot
            factors.append(THROUGH_CONDUCT * inverse)
            values.append(right * inverse)
        return factors, values

    middle = layers // 2
    low_f, low_v = sweep(range(middle))
    high_f, high_v = sweep(range(layers - 1, middle - 1, -1))
    low = (low_v[-1] + low_f[-1] * high_v[-1]) / (1.0 - low_f[-1] * high_f[-1])
    high = high_v[-1] + high_f[-1] * low
    heat_new[0, middle - 1] = low
    heat_new[0, middle] = high
    for step in range(middle - 2, -1, -1):
        low = low_v[step] + low_f[step] * low
        heat_new[0, step] = low
    for step in range(len(high_v) - 2, -1, -1):
        high = high_v[step] + high_f[step] * high
        heat_new[0, layers - 1 - step] = high
    heat_write = pltpu.make_async_copy(heat_new, heat_out, sem.at[slots])
    heat_write.start()
    for write in writes:
        write.wait()
    heat_write.wait()


def per_device(cells, subs, shell_conc, heat_rise, layer_current, layer_counts, contacts):
    _, slots, shells, gy, gx = shell_conc.shape
    _, layers, rows, _ = heat_rise.shape
    f32 = jnp.float32
    dma = pltpu.SemaphoreType.DMA
    table = (layers, rows, gx)
    held = [
        pltpu.with_memory_space_constraint(array, pltpu.HBM)
        for array in (layer_counts, contacts.T, heat_rise, shell_conc, layer_current)
    ]
    conc, right_side, pivots = pl.pallas_call(
        functools.partial(kernel, cells, subs),
        out_shape=(
            pltpu.VMEM((slots, shells, gy, gx), f32),
            pltpu.VMEM(table, f32),
            pltpu.VMEM(table, f32),
        ),
        in_specs=[
            pl.BlockSpec(memory_space=pltpu.HBM)
        ] * 5,
        out_specs=(pl.BlockSpec(memory_space=pltpu.VMEM),) * 3,
        scratch_shapes=[
            pltpu.VMEM(heat_rise.shape, f32),
            pltpu.VMEM((subs * slots, rows, gx), f32),
            pltpu.VMEM((slots, gy, gx), f32),
            pltpu.VMEM((slots, gy, gx), f32),
            pltpu.VMEM((subs * slots, rows, gx), f32),
            pltpu.VMEM((subs * slots, rows, gx), f32),
            pltpu.VMEM((2, layers, gx), f32),
            pltpu.VMEM((layers, gx), f32),
            pltpu.VMEM((layers, gx), f32),
            pltpu.VMEM((cells, 2, rows, gx), f32),
            pltpu.VMEM(table, f32),
            pltpu.VMEM((subs * slots, rows, gx), f32),
            pltpu.VMEM((subs * slots, rows, gx), f32),
            pltpu.SMEM((layers,), jnp.int32),
            pltpu.SMEM(layer_counts.shape, jnp.int32),
            pltpu.SMEM(contacts.shape[::-1], jnp.int32),
            pltpu.SemaphoreType.REGULAR((2, max(subs // PAIR, 2))),
            pltpu.SemaphoreType.REGULAR((2, max(cells.bit_length() - 1, 1))),
            dma((7,)),
            dma((subs,)),
            dma((subs,)),
            dma((subs,)),
            dma((subs,)),
            dma((subs,)),
            dma((subs,)),
            dma((2,)),
            dma((2,)),
            dma((2 * cells,)),
            dma((2 * cells,)),
        ],
        compiler_params=pltpu.CompilerParams(
            collective_id=0, has_side_effects=True, vmem_limit_bytes=GRANT
        ),
    )(*held)
    conc_new, heat_new = pl.pallas_call(
        finish,
        out_shape=(
            jax.ShapeDtypeStruct(shell_conc.shape, f32),
            jax.ShapeDtypeStruct(heat_rise.shape, f32),
        ),
        in_specs=[pl.BlockSpec(memory_space=pltpu.VMEM)] * 3,
        out_specs=(
            pl.BlockSpec(memory_space=pl.ANY),
            pl.BlockSpec(memory_space=pl.ANY),
        ),
        scratch_shapes=[pltpu.VMEM(heat_rise.shape, f32), dma((slots + 1,))],
        compiler_params=pltpu.CompilerParams(vmem_limit_bytes=GRANT),
    )(conc, right_side, pivots)
    return conc_new, heat_new


def solution(mesh):
    in_specs = (
        P("cell", "sub", None, None, None),
        P("cell", None, "sub", None),
        P("cell", "sub", None, None),
        P(),
        P(),
    )
    out_specs = (P("cell", "sub", None, None, None), P("cell", None, "sub", None))
    body = functools.partial(per_device, mesh.shape["cell"], mesh.shape["sub"])
    return jax.shard_map(
        body, mesh=mesh, in_specs=in_specs, out_specs=out_specs, check_vma=False
    )
```

```python
import functools

import jax
import jax.numpy as jnp
from jax import lax
from jax.experimental import pallas as pl
from jax.experimental.pallas import tpu as pltpu
from jax.sharding import PartitionSpec as P

BASE_KELVIN = 298.15
RATE_ACTIVATION = 5000.0
DIFFUSION_ACTIVATION = 3000.0
RATE_CONSTANT = 0.5
VOLT_PER_KELVIN = 2.0 * 8.314462618 / 96485.33212
HEAT_SCALE = 10.0
ENTROPY_SLOPE = 0.001
DIFFUSION_STEP = 0.005
SURFACE_STEP = 0.005
INPLANE_CONDUCT = 0.25
THROUGH_CONDUCT = 2.0
CONTACT_CONDUCT = 0.5
MESH = pl.DeviceIdType.MESH
GRANT = 24 << 20
PAIR = 2


def partner(me, offset):
    bit = 1
    result = me
    while bit <= offset:
        if offset & bit:
            result = result + bit * (1 - 2 * ((me // bit) % 2))
        bit *= 2
    return result


def inverse_sine(value):
    magnitude = jnp.abs(value)
    rooted = jnp.sqrt(1.0 + magnitude * magnitude)
    positive = jnp.log1p(magnitude + magnitude * magnitude / (1.0 + rooted))
    return jnp.where(value < 0.0, -positive, positive), rooted


def kinetics(surface, rise, current):
    kelvin = BASE_KELVIN + rise
    per_kelvin = 1.0 / kelvin
    reciprocal = rise * (1.0 / BASE_KELVIN) * per_kelvin
    ratio_rate = (
        current
        * jnp.exp(-RATE_ACTIVATION * reciprocal)
        * lax.rsqrt(surface * (1.0 - surface))
        * (0.5 / RATE_CONSTANT)
    )
    arcsine, rooted = inverse_sine(ratio_rate)
    entropic = ENTROPY_SLOPE * (0.5 - surface)
    scaled = HEAT_SCALE * current
    common = VOLT_PER_KELVIN * arcsine + entropic
    source = scaled * kelvin * common
    heat_slope = scaled * (
        common - (VOLT_PER_KELVIN * RATE_ACTIVATION) * ratio_rate * per_kelvin / rooted
    )
    return source, heat_slope


def kernel(
    cells, subs,
    counts_hbm, contacts_hbm, heat_hbm, conc, current,
    conc_in, answer,
    heat, staged, slot_rise, current_in, surface_rows, current_rows,
    edges, low_edge, high_edge, faces, base, extra, diagonal, layer_slot, slot_layer, counts, contacts,
    twin_out, twin_in, solved, factors, values, contact_out, contact_in, match_out, match_in, part, border_out, border_in,
    reach, cell_reach, own_sem, heat_send, heat_recv, surf_send, surf_recv, curr_send, curr_recv,
    edge_send, edge_recv, face_send, face_recv,
    twin_send, twin_recv, pair_send, pair_recv, border_send, border_recv,
):
    cell = lax.axis_index("cell")
    sub = lax.axis_index("sub")
    slots, shells, gy, gx = conc_in.shape
    layers, rows, _ = heat.shape[1:]

    offsets = list(range(1, subs))
    arrivals = offsets[: PAIR - 1] + offsets[2 * PAIR - 2 : PAIR - 2 : -1] + offsets[: 2 * PAIR - 2 : -1]
    chip, core, chips = sub // PAIR, sub % PAIR, subs // PAIR
    cell_bits = [1 << bit for bit in range(cells.bit_length() - 1)]

    half = subs // 2
    own_slots = half * slots
    left = 2 * chip < chips
    ours = jnp.where(left, chips // 2 - 1, chips // 2)
    theirs = chips - 1 - ours
    own_first = jnp.where(left, 0, own_slots)
    other_first = own_slots - own_first
    twin = theirs * PAIR + core

    def has_chip(shift):
        return jnp.logical_and(chip + shift >= 0, chip + shift < chips)

    def on_chip(shift, place):
        return jnp.clip(chip + shift, 0, chips - 1) * PAIR + place

    def at_sub(index):
        return (cell, index)

    first_loads = [
        pltpu.make_async_copy(counts_hbm, counts, own_sem.at[5]),
        pltpu.make_async_copy(heat_hbm, heat, own_sem.at[4]),
        pltpu.make_async_copy(contacts_hbm, contacts, own_sem.at[6]),
    ]
    for load in first_loads:
        load.start()
    barrier = pltpu.get_barrier_semaphore()

    def greet(device):
        pl.semaphore_signal(barrier, inc=1, device_id=device, device_id_type=MESH)

    for place in range(1, PAIR):
        greet(at_sub(chip * PAIR + (core + place) % PAIR))
    inward = jnp.where(2 * chip < chips, 1, -1)
    middle = jnp.logical_or(chip == chips // 2 - 1, chip == chips // 2)
    for shift in (-1, 1):

        @pl.when(jnp.logical_and(has_chip(shift), jnp.logical_or(inward != shift, middle)))
        def _():
            for place in range(PAIR):
                greet(at_sub(on_chip(shift, place)))

    for bit in cell_bits:

        @pl.when((cell // bit) % 2 == 0)
        def _():
            greet((partner(cell, bit), sub))

    loads = [
        pltpu.make_async_copy(current.at[0], current_in, own_sem.at[0]),
        pltpu.make_async_copy(conc.at[0], conc_in, own_sem.at[1]),
    ]
    for load in loads:
        load.start()

    lower = sum((cell // bit) % 2 for bit in cell_bits)
    pl.semaphore_wait(barrier, PAIR - 1 + (PAIR if chips > 1 else 0) + lower)

    def tell(semaphore, device):
        pl.semaphore_signal(semaphore, inc=1, device_id=device, device_id_type=MESH)

    for way, shift in enumerate((1, -1)):

        @pl.when(jnp.logical_and(inward == -shift, jnp.logical_not(middle)))
        def _():
            tell(reach.at[way, 0], at_sub(on_chip(-shift, core)))

    for place, bit in enumerate(cell_bits):

        @pl.when((cell // bit) % 2 == 1)
        def _():
            tell(cell_reach.at[0, place], (partner(cell, bit), sub))

    def relay(distance):
        for way, shift in enumerate((1, -1)):

            @pl.when(jnp.logical_and(has_chip(-shift), has_chip(shift * (distance - 1))))
            def _():
                tell(reach.at[way, distance - 1], at_sub(on_chip(-shift, core)))

    def learn(distance):
        for way, shift in enumerate((1, -1)):

            known = has_chip(shift * distance)
            if distance == 1:
                known = jnp.logical_and(known, inward != shift)

            @pl.when(known)
            def _():
                pl.semaphore_wait(reach.at[way, distance - 1], 1)

    sends = []

    def rows_of(index):
        return pl.ds(pl.multiple_of(index * rows, rows), rows)

    def slots_of(index):
        return pl.ds(index * slots, slots)

    def heat_copy(source, target, device):
        return pltpu.make_async_remote_copy(
            src_ref=staged.at[slots_of(target)],
            dst_ref=slot_rise.at[:, rows_of(source)],
            send_sem=heat_send.at[target],
            recv_sem=heat_recv.at[source],
            device_id=at_sub(device),
            device_id_type=MESH,
        )

    def surf_copy(source, target, device):
        return pltpu.make_async_remote_copy(
            src_ref=conc.at[0, :, shells - 1, rows_of(target)],
            dst_ref=surface_rows.at[slots_of(source)],
            send_sem=surf_send.at[target],
            recv_sem=surf_recv.at[source],
            device_id=at_sub(device),
            device_id_type=MESH,
        )

    def curr_copy(source, target, device):
        return pltpu.make_async_remote_copy(
            src_ref=current.at[0, :, rows_of(target)],
            dst_ref=current_rows.at[slots_of(source)],
            send_sem=curr_send.at[target],
            recv_sem=curr_recv.at[source],
            device_id=at_sub(device),
            device_id_type=MESH,
        )

    inner = jnp.logical_and(has_chip(-1), has_chip(1))
    outer = jnp.logical_not(inner)

    def issue(distance, makers, when=True, within=None):
        for shift in (distance, -distance) if distance else (0,):

            wanted = jnp.logical_and(has_chip(shift), when)
            if distance and heat_copy not in makers:
                crossing = jnp.logical_and(chip + shift == theirs, distance > 0)
                wanted = jnp.logical_and(wanted, jnp.logical_not(crossing))
            if within is not None:
                wanted = jnp.logical_and(wanted, (inward == shift) == within)

            @pl.when(wanted)
            def _():
                for make in makers:
                    for place in range(PAIR) if distance else range(1, PAIR):
                        other = on_chip(shift, place if distance else (core + place) % PAIR)
                        make(sub, other, other).start()

    issue(1, (curr_copy, surf_copy), outer)
    for load in first_loads:
        load.wait()
    edges[0] = heat[0, :, 0]
    edges[1] = heat[0, :, rows - 1]
    start = jnp.int32(0)
    for index in range(subs):
        held = counts[index]
        for place in range(slots):
            layer = jnp.minimum(start + place, layers - 1)
            staged[index * slots + place] = heat[0, layer]
            slot_layer[index * slots + place] = layer
            border_out[index, place] = heat[0, layer, jnp.where(left, rows - 1, 0)]
        start = start + held
    faces[cell] = jnp.zeros((2, rows, gx), jnp.float32)

    issue(1, (heat_copy,), within=True)
    learn(1)
    if chips > 2:
        relay(2)
    issue(1, (heat_copy,), within=False)
    issue(0, (heat_copy, surf_copy, curr_copy))
    to_below = pltpu.make_async_remote_copy(
        src_ref=edges.at[0],
        dst_ref=high_edge,
        send_sem=edge_send.at[0],
        recv_sem=edge_recv.at[0],
        device_id=at_sub(jnp.maximum(sub - 1, 0)),
        device_id_type=MESH,
    )
    to_above = pltpu.make_async_remote_copy(
        src_ref=edges.at[1],
        dst_ref=low_edge,
        send_sem=edge_send.at[1],
        recv_sem=edge_recv.at[1],
        device_id=at_sub(jnp.minimum(sub + 1, subs - 1)),
        device_id_type=MESH,
    )

    @pl.when(sub > 0)
    def _():
        to_below.start()

    @pl.when(sub < subs - 1)
    def _():
        to_above.start()

    far = range(chips - 1, 1, -1)
    for distance in range(2, chips):
        learn(distance)
        if distance + 1 < chips:
            relay(distance + 1)
    bordering = jnp.logical_and(
        chip == ours + jnp.where(left, -1, 1), core == jnp.where(left, PAIR - 1, 0)
    )

    def border_copy(target):
        return pltpu.make_async_remote_copy(
            src_ref=border_out.at[target],
            dst_ref=border_in,
            send_sem=border_send.at[target],
            recv_sem=border_recv.at[0],
            device_id=at_sub(target),
            device_id_type=MESH,
        )

    def borders(act):
        @pl.when(bordering)
        def _():
            for place in range(half):
                act(border_copy(jnp.where(left, half + place, place)))

    borders(lambda copy: copy.start())
    for distance in far:
        issue(distance, (heat_copy,))
    for distance in far:
        issue(distance, (surf_copy, curr_copy), inner)
    for distance in far:
        issue(distance, (surf_copy,), jnp.logical_and(outer, left))

    def face_copies(source, device):
        return [
            pltpu.make_async_remote_copy(
                src_ref=heat_hbm.at[0, layer],
                dst_ref=faces.at[source, place],
                send_sem=face_send.at[2 * device + place],
                recv_sem=face_recv.at[2 * source + place],
                device_id=(device, sub),
                device_id_type=MESH,
            )
            for place, layer in ((0, 0), (1, layers - 1))
        ]

    for place, bit in enumerate(cell_bits):

        @pl.when((cell // bit) % 2 == 0)
        def _():
            pl.semaphore_wait(cell_reach.at[0, place], 1)

    def spread(place):
        tell(cell_reach.at[1, place], (partner(cell, cell_bits[place]), sub))

    if len(cell_bits) > 1:
        spread(0)

    def send_faces():
        for place in range(len(cell_bits) - 1):
            pl.semaphore_wait(cell_reach.at[1, place], 1)
            if place + 1 < len(cell_bits) - 1:
                spread(place + 1)
        for offset in range(1, cells):
            for copy in face_copies(cell, partner(cell, offset)):
                copy.start()
                sends.append(copy)


    mine = [
        pltpu.make_async_copy(
            conc.at[0, :, shells - 1, rows_of(sub)], surface_rows.at[slots_of(sub)], own_sem.at[2]
        ),
        pltpu.make_async_copy(
            current.at[0, :, rows_of(sub)], current_rows.at[slots_of(sub)], own_sem.at[3]
        ),
    ]
    for copy in mine:
        copy.start()
    slot_rise[:, rows_of(sub)] = staged[slots_of(sub)]

    def slot_of(layer, carry):
        total = jnp.int32(0)
        slot = layer
        for index in range(subs):
            total = total + counts[index]
            slot = slot + jnp.where(total <= layer, slots - counts[index], 0)
        layer_slot[layer] = jnp.minimum(slot, subs * slots - 1)
        return carry

    lax.fori_loop(0, layers, slot_of, jnp.int32(0))

    live_count = counts[sub]
    live = lax.broadcasted_iota(jnp.int32, (slots, rows, gx), 0) < live_count
    volumes = [((r + 1) ** 3 - r**3) / (3.0 * shells**3) for r in range(shells)]
    weights = [DIFFUSION_STEP * ((r + 1) ** 2 / shells**2 * shells) for r in range(shells - 1)]

    def particle(where):
        rise = slot_rise[:, where]
        speedup = jnp.exp(
            (DIFFUSION_ACTIVATION / BASE_KELVIN) * rise / (BASE_KELVIN + rise)
        )
        uppers = []
        values = []
        link = None
        for r in range(shells):
            right = volumes[r] * conc_in[:, r, where]
            if r == shells - 1:
                right = right - SURFACE_STEP * current_in[:, where]
            pivot = volumes[r]
            if r > 0:
                pivot = pivot + link * (1.0 - uppers[r - 1])
                right = right + link * values[r - 1]
            if r < shells - 1:
                next_link = weights[r] * speedup
                pivot = pivot + next_link
            inverse = 1.0 / pivot
            if r < shells - 1:
                uppers.append(next_link * inverse)
                link = next_link
            values.append(right * inverse)
        result = values[shells - 1]
        conc_in[:, shells - 1, where] = jnp.where(live, result, 0.0)
        for r in range(shells - 2, -1, -1):
            result = values[r] + uppers[r] * result
            conc_in[:, r, where] = jnp.where(live, result, 0.0)

    for load in loads:
        load.wait()
    near = [0] + arrivals[: 2 * PAIR - 1]
    rest = arrivals[2 * PAIR - 1 :]
    for count, offset in enumerate(near):
        other = partner(sub, offset)
        if offset:
            heat_copy(other, sub, other).wait_recv()
        particle(rows_of(other))
        if count == 0:
            send_faces()
        if count == 1:
            issue(1, (surf_copy, curr_copy), inner)
    row_index = lax.broadcasted_iota(jnp.int32, (rows, gx), 0)
    lane_index = lax.broadcasted_iota(jnp.int32, (rows, gx), 1)

    def smoothed(here, before, after):
        up = jnp.where(row_index == 0, before, pltpu.roll(here, 1, 0))
        down = jnp.where(row_index == rows - 1, after, pltpu.roll(here, rows - 1, 0))
        left_side = jnp.where(lane_index == 0, here, pltpu.roll(here, 1, 1))
        right_side = jnp.where(lane_index == gx - 1, here, pltpu.roll(here, gx - 1, 1))
        return here + INPLANE_CONDUCT * (down + up + right_side + left_side - 4.0 * here)

    def twin_copy(source, place):
        return pltpu.make_async_remote_copy(
            src_ref=twin_out.at[place],
            dst_ref=twin_in.at[:, slots_of(source % half)],
            send_sem=twin_send.at[place],
            recv_sem=twin_recv.at[source % half],
            device_id=at_sub(ours * PAIR + place),
            device_id_type=MESH,
        )

    def heat_from(chip_index):
        for place in range(PAIR):
            other = chip_index * PAIR + place
            heat_copy(other, sub, other).wait_recv()

    heat_from(theirs)
    border_copy(sub).wait_recv()
    for count in range(PAIR):
        place = jnp.where(left, count, PAIR - 1 - count)
        index = theirs * PAIR + place
        here = slot_rise[:, rows_of(index)]
        source, slope = kinetics(
            conc_in[:, shells - 1, rows_of(index)], here, current_in[:, rows_of(index)]
        )
        extra_here = source - slope * here
        for s in range(slots):
            first, last = index * rows, index * rows + rows - 1
            open_low = jnp.logical_and(jnp.logical_not(left), place == 0)
            open_high = jnp.logical_and(left, place == PAIR - 1)
            before = slot_rise[s, pl.ds(jnp.where(open_low, first, first - 1), 1)]
            after = slot_rise[s, pl.ds(jnp.where(open_high, last, last + 1), 1)]
            rim = border_in[pl.ds(s, 1)]
            before = jnp.where(open_low, rim, before)
            after = jnp.where(open_high, rim, after)
            twin_out[place, 0, s] = smoothed(here[s], before, after) + extra_here[s]
        twin_out[place, 1] = 1.0 - slope
        mine_too = sub == ours * PAIR + place

        @pl.when(mine_too)
        def _():
            twin_in[:, slots_of(sub % half)] = twin_out[place]

        @pl.when(jnp.logical_not(mine_too))
        def _():
            twin_copy(sub, place).start()

    for distance in far:
        issue(distance, (surf_copy,), jnp.logical_and(outer, jnp.logical_not(left)))
    for distance in far:
        issue(distance, (curr_copy,), outer)

    @pl.when(sub > 0)
    def _():
        to_above.wait_recv()

    @pl.when(sub == 0)
    def _():
        low_edge[...] = edges[0]

    @pl.when(sub < subs - 1)
    def _():
        to_below.wait_recv()

    @pl.when(sub == subs - 1)
    def _():
        high_edge[...] = edges[1]

    for offset in range(1, cells):
        other = partner(cell, offset)
        for copy in face_copies(other, other):
            copy.wait_recv()

    def fill(layer, carry):
        base[layer] = smoothed(heat[0, layer], low_edge[pl.ds(layer, 1)], high_edge[pl.ds(layer, 1)])
        return carry

    lax.fori_loop(0, layers, fill, jnp.int32(0), unroll=2)
    lower_cell = contacts[0, cell]
    upper_cell = contacts[1, cell]
    below_face = jnp.where(lower_cell >= 0, faces[jnp.maximum(lower_cell, 0), 1], 0.0)
    above_face = jnp.where(upper_cell >= 0, faces[jnp.maximum(upper_cell, 0), 0], 0.0)
    share = CONTACT_CONDUCT / THROUGH_CONDUCT
    low_start = share * (below_face - heat[0, 0])
    high_start = share * (above_face - heat[0, layers - 1])
    own_start = jnp.where(left, low_start, high_start)
    other_start = jnp.where(left, high_start, low_start)

    def pair_copy(index, source, target):
        return pltpu.make_async_remote_copy(
            src_ref=source,
            dst_ref=target,
            send_sem=pair_send.at[index],
            recv_sem=pair_recv.at[index],
            device_id=at_sub(twin),
            device_id_type=MESH,
        )

    contact_copy = pair_copy(0, contact_out, contact_in)
    match_copy = pair_copy(1, match_out, match_in)
    part_copy = pair_copy(2, part, solved.at[pl.ds(own_first, own_slots)])

    @pl.when(middle)
    def _():
        contact_out[...] = other_start
        contact_copy.start()

    def prepare(offset):
        other = partner(sub, offset)
        if offset:
            surf_copy(other, sub, other).wait_recv()
            curr_copy(other, sub, other).wait_recv()
        else:
            for copy in mine:
                copy.wait()
        at = slots_of(other)
        rise = staged[at]
        source, slope = kinetics(surface_rows[at], rise, current_rows[at])
        extra[at] = source - slope * rise
        diagonal[at] = 1.0 - slope

    def eliminate(bank, low, fetch, start):
        pivot = jnp.full((rows, gx), 1.0, jnp.float32)
        before = jnp.full((rows, gx), 0.5, jnp.float32)
        total = start
        for step in range(own_slots):
            index = jnp.where(low, step, own_slots - 1 - step)
            owner = jnp.where(low, step // slots, subs - 1 - step // slots)
            filled = jnp.where(low, step % slots, slots - 1 - step % slots) < counts[owner]
            right, own = fetch(index)
            own = own + 2.0 * THROUGH_CONDUCT
            next_pivot = own * pivot - THROUGH_CONDUCT**2 * before
            next_total = right * pivot + THROUGH_CONDUCT * total
            inverse = 1.0 / next_pivot
            factors[bank, step] = jnp.where(filled, THROUGH_CONDUCT * pivot * inverse, 1.0)
            values[bank, step] = jnp.where(filled, next_total * inverse, 0.0)
            before = jnp.where(filled, pivot, before)
            pivot = jnp.where(filled, next_pivot, pivot)
            total = jnp.where(filled, next_total, total)
        inverse = 1.0 / pivot
        return THROUGH_CONDUCT * before * inverse, total * inverse

    def unwind(bank, low, result, target, first):
        for step in range(own_slots - 1, -1, -1):
            result = values[bank, step] + factors[bank, step] * result
            target[first + jnp.where(low, step, own_slots - 1 - step)] = result

    def from_rows(first):
        def fetch(index):
            slot = first + index
            return base[slot_layer[slot]] + extra[slot], diagonal[slot]

        return fetch

    def meeting(factor, value, other_factor, other_value):
        return (other_value + other_factor * value) / (1.0 - factor * other_factor)

    for offset in [0] + arrivals:
        if offset < half:
            prepare(offset)
    own_factor, own_value = eliminate(0, left, from_rows(own_first), own_start)

    @pl.when(middle)
    def _():
        match_out[0] = own_factor
        match_out[1] = own_value
        match_copy.start()
        for place in range(half):
            source = jnp.where(left, place, half + place)

            @pl.when(source != sub)
            def _():
                twin_copy(source, 0).wait_recv()

        contact_copy.wait_recv()
        factor, value = eliminate(
            1, left, lambda index: (twin_in[0, index], twin_in[1, index]), contact_in[...]
        )
        match_copy.wait_recv()
        unwind(1, left, meeting(factor, value, match_in[0], match_in[1]), part, 0)
        part_copy.start()

    for offset in rest:
        other = partner(sub, offset)

        @pl.when(other // PAIR != theirs)
        def _():
            heat_copy(other, sub, other).wait_recv()

        particle(rows_of(other))

    @pl.when(middle)
    def _():
        part_copy.wait_recv()
        rim = solved[jnp.where(left, own_slots, own_slots - slots)]
        for place in range(1, slots):
            beyond = solved[jnp.where(left, own_slots, own_slots - slots + place)]
            rim = jnp.where(counts[half - 1] > place, beyond, rim)
        unwind(0, left, rim, solved, own_first)
        contact_copy.wait_send()
        match_copy.wait_send()
        part_copy.wait_send()

    @pl.when(jnp.logical_not(middle))
    def _():
        for offset in arrivals:
            if offset >= half:
                prepare(offset)
        right = jnp.logical_not(left)
        factor, value = eliminate(1, right, from_rows(other_first), other_start)
        across = meeting(own_factor, own_value, factor, value)
        unwind(0, left, across, solved, own_first)
        back = meeting(factor, value, own_factor, own_value)
        unwind(1, right, back, solved, other_first)

    borders(lambda copy: copy.wait_send())
    for layer in range(layers):
        answer[0, layer] = solved[layer_slot[layer]]

    for place in range(PAIR):

        @pl.when(sub != ours * PAIR + place)
        def _():
            twin_copy(sub, place).wait_send()

    for offset in offsets:
        other = partner(sub, offset)
        heat_copy(sub, other, other).wait_send()

        @pl.when(jnp.logical_or(other // PAIR != theirs, offset < half))
        def _():
            surf_copy(sub, other, other).wait_send()
            curr_copy(sub, other, other).wait_send()

    for copy in sends:
        copy.wait_send()

    @pl.when(sub > 0)
    def _():
        to_below.wait_send()

    @pl.when(sub < subs - 1)
    def _():
        to_above.wait_send()


def finish(conc, answer, conc_new, heat_new, sem):
    slots = conc.shape[0]
    writes = [
        pltpu.make_async_copy(conc.at[s], conc_new.at[0, s], sem.at[s]) for s in range(slots)
    ]
    writes.append(pltpu.make_async_copy(answer, heat_new, sem.at[slots]))
    for write in writes:
        write.start()
    for write in writes:
        write.wait()


def per_device(cells, subs, shell_conc, heat_rise, layer_current, layer_counts, contacts):
    _, slots, shells, gy, gx = shell_conc.shape
    _, layers, rows, _ = heat_rise.shape
    f32 = jnp.float32
    dma = pltpu.SemaphoreType.DMA
    table = (layers, rows, gx)
    own_slots = subs // 2 * slots
    held = [
        pltpu.with_memory_space_constraint(array, pltpu.HBM)
        for array in (layer_counts, contacts.T, heat_rise, shell_conc, layer_current)
    ]
    conc, answer = pl.pallas_call(
        functools.partial(kernel, cells, subs),
        out_shape=(
            pltpu.VMEM((slots, shells, gy, gx), f32),
            pltpu.VMEM(heat_rise.shape, f32),
        ),
        in_specs=[
            pl.BlockSpec(memory_space=pltpu.HBM)
        ] * 5,
        out_specs=(pl.BlockSpec(memory_space=pltpu.VMEM),) * 2,
        scratch_shapes=[
            pltpu.VMEM(heat_rise.shape, f32),
            pltpu.VMEM((subs * slots, rows, gx), f32),
            pltpu.VMEM((slots, gy, gx), f32),
            pltpu.VMEM((slots, gy, gx), f32),
            pltpu.VMEM((subs * slots, rows, gx), f32),
            pltpu.VMEM((subs * slots, rows, gx), f32),
            pltpu.VMEM((2, layers, gx), f32),
            pltpu.VMEM((layers, gx), f32),
            pltpu.VMEM((layers, gx), f32),
            pltpu.VMEM((cells, 2, rows, gx), f32),
            pltpu.VMEM(table, f32),
            pltpu.VMEM((subs * slots, rows, gx), f32),
            pltpu.VMEM((subs * slots, rows, gx), f32),
            pltpu.SMEM((layers,), jnp.int32),
            pltpu.SMEM((subs * slots,), jnp.int32),
            pltpu.SMEM(layer_counts.shape, jnp.int32),
            pltpu.SMEM(contacts.shape[::-1], jnp.int32),
            pltpu.VMEM((PAIR, 2, slots, rows, gx), f32),
            pltpu.VMEM((2, own_slots, rows, gx), f32),
            pltpu.VMEM((subs * slots, rows, gx), f32),
            pltpu.VMEM((2, own_slots, rows, gx), f32),
            pltpu.VMEM((2, own_slots, rows, gx), f32),
            pltpu.VMEM((rows, gx), f32),
            pltpu.VMEM((rows, gx), f32),
            pltpu.VMEM((2, rows, gx), f32),
            pltpu.VMEM((2, rows, gx), f32),
            pltpu.VMEM((own_slots, rows, gx), f32),
            pltpu.VMEM((subs, slots, gx), f32),
            pltpu.VMEM((slots, gx), f32),
            pltpu.SemaphoreType.REGULAR((2, max(subs // PAIR, 2))),
            pltpu.SemaphoreType.REGULAR((2, max(cells.bit_length() - 1, 1))),
            dma((7,)),
            dma((subs,)),
            dma((subs,)),
            dma((subs,)),
            dma((subs,)),
            dma((subs,)),
            dma((subs,)),
            dma((2,)),
            dma((2,)),
            dma((2 * cells,)),
            dma((2 * cells,)),
            dma((PAIR,)),
            dma((subs // 2,)),
            dma((3,)),
            dma((3,)),
            dma((subs,)),
            dma((1,)),
        ],
        compiler_params=pltpu.CompilerParams(
            collective_id=0, has_side_effects=True, vmem_limit_bytes=GRANT
        ),
    )(*held)
    conc_new, heat_new = pl.pallas_call(
        finish,
        out_shape=(
            jax.ShapeDtypeStruct(shell_conc.shape, f32),
            jax.ShapeDtypeStruct(heat_rise.shape, f32),
        ),
        in_specs=[pl.BlockSpec(memory_space=pltpu.VMEM)] * 2,
        out_specs=(
            pl.BlockSpec(memory_space=pl.ANY),
            pl.BlockSpec(memory_space=pl.ANY),
        ),
        scratch_shapes=[dma((slots + 1,))],
        compiler_params=pltpu.CompilerParams(vmem_limit_bytes=GRANT),
    )(conc, answer)
    return conc_new, heat_new


def solution(mesh):
    in_specs = (
        P("cell", "sub", None, None, None),
        P("cell", None, "sub", None),
        P("cell", "sub", None, None),
        P(),
        P(),
    )
    out_specs = (P("cell", "sub", None, None, None), P("cell", None, "sub", None))
    body = functools.partial(per_device, mesh.shape["cell"], mesh.shape["sub"])
    return jax.shard_map(
        body, mesh=mesh, in_specs=in_specs, out_specs=out_specs, check_vma=False
    )
```

```python
import functools

import jax
import jax.numpy as jnp
from jax import lax
from jax.experimental import pallas as pl
from jax.experimental.pallas import tpu as pltpu
from jax.sharding import PartitionSpec as P

BASE_KELVIN = 298.15
RATE_ACTIVATION = 5000.0
DIFFUSION_ACTIVATION = 3000.0
RATE_CONSTANT = 0.5
VOLT_PER_KELVIN = 2.0 * 8.314462618 / 96485.33212
HEAT_SCALE = 10.0
ENTROPY_SLOPE = 0.001
DIFFUSION_STEP = 0.005
SURFACE_STEP = 0.005
INPLANE_CONDUCT = 0.25
THROUGH_CONDUCT = 2.0
CONTACT_CONDUCT = 0.5
MESH = pl.DeviceIdType.MESH
GRANT = 24 << 20
PAIR = 2


def partner(me, offset):
    bit = 1
    result = me
    while bit <= offset:
        if offset & bit:
            result = result + bit * (1 - 2 * ((me // bit) % 2))
        bit *= 2
    return result


def inverse_sine(value):
    magnitude = jnp.abs(value)
    rooted = jnp.sqrt(1.0 + magnitude * magnitude)
    positive = jnp.log1p(magnitude + magnitude * magnitude / (1.0 + rooted))
    return jnp.where(value < 0.0, -positive, positive), rooted


def kinetics(surface, rise, current):
    kelvin = BASE_KELVIN + rise
    per_kelvin = 1.0 / kelvin
    reciprocal = rise * (1.0 / BASE_KELVIN) * per_kelvin
    ratio_rate = (
        current
        * jnp.exp(-RATE_ACTIVATION * reciprocal)
        * lax.rsqrt(surface * (1.0 - surface))
        * (0.5 / RATE_CONSTANT)
    )
    arcsine, rooted = inverse_sine(ratio_rate)
    entropic = ENTROPY_SLOPE * (0.5 - surface)
    scaled = HEAT_SCALE * current
    common = VOLT_PER_KELVIN * arcsine + entropic
    source = scaled * kelvin * common
    heat_slope = scaled * (
        common - (VOLT_PER_KELVIN * RATE_ACTIVATION) * ratio_rate * per_kelvin / rooted
    )
    return source, heat_slope


def kernel(
    cells, subs,
    counts_hbm, contacts_hbm, heat_hbm, conc, current,
    conc_in, answer,
    heat, staged, slot_rise, current_in, surface_rows, current_rows,
    edges, low_edge, high_edge, faces, base, extra, diagonal, layer_slot, slot_layer, counts, contacts,
    twin_out, twin_in, solved, factors, values, contact_out, contact_in, match_out, match_in, part, border_out, border_in,
    reach, cell_reach, own_sem, heat_send, heat_recv, surf_send, surf_recv, curr_send, curr_recv,
    edge_send, edge_recv, face_send, face_recv,
    twin_send, twin_recv, pair_send, pair_recv, border_send, border_recv,
):
    cell = lax.axis_index("cell")
    sub = lax.axis_index("sub")
    slots, shells, gy, gx = conc_in.shape
    layers, rows, _ = heat.shape[1:]

    offsets = list(range(1, subs))
    arrivals = offsets[: PAIR - 1] + offsets[2 * PAIR - 2 : PAIR - 2 : -1] + offsets[: 2 * PAIR - 2 : -1]
    chip, core, chips = sub // PAIR, sub % PAIR, subs // PAIR
    cell_bits = [1 << bit for bit in range(cells.bit_length() - 1)]

    half = subs // 2
    own_slots = half * slots
    left = 2 * chip < chips
    ours = jnp.where(left, chips // 2 - 1, chips // 2)
    theirs = chips - 1 - ours
    own_first = jnp.where(left, 0, own_slots)
    other_first = own_slots - own_first
    twin = theirs * PAIR + core

    def has_chip(shift):
        return jnp.logical_and(chip + shift >= 0, chip + shift < chips)

    def on_chip(shift, place):
        return jnp.clip(chip + shift, 0, chips - 1) * PAIR + place

    def at_sub(index):
        return (cell, index)

    first_loads = [
        pltpu.make_async_copy(counts_hbm, counts, own_sem.at[5]),
        pltpu.make_async_copy(heat_hbm, heat, own_sem.at[4]),
        pltpu.make_async_copy(contacts_hbm, contacts, own_sem.at[6]),
    ]
    for load in first_loads:
        load.start()
    barrier = pltpu.get_barrier_semaphore()

    def greet(device):
        pl.semaphore_signal(barrier, inc=1, device_id=device, device_id_type=MESH)

    for place in range(1, PAIR):
        greet(at_sub(chip * PAIR + (core + place) % PAIR))
    inward = jnp.where(2 * chip < chips, 1, -1)
    middle = jnp.logical_or(chip == chips // 2 - 1, chip == chips // 2)
    for shift in (-1, 1):

        @pl.when(jnp.logical_and(has_chip(shift), jnp.logical_or(inward != shift, middle)))
        def _():
            for place in range(PAIR):
                greet(at_sub(on_chip(shift, place)))

    for bit in cell_bits:

        @pl.when((cell // bit) % 2 == 0)
        def _():
            greet((partner(cell, bit), sub))

    loads = [
        pltpu.make_async_copy(current.at[0], current_in, own_sem.at[0]),
        pltpu.make_async_copy(conc.at[0], conc_in, own_sem.at[1]),
    ]
    for load in loads:
        load.start()

    lower = sum((cell // bit) % 2 for bit in cell_bits)
    pl.semaphore_wait(barrier, PAIR - 1 + (PAIR if chips > 1 else 0) + lower)

    def tell(semaphore, device):
        pl.semaphore_signal(semaphore, inc=1, device_id=device, device_id_type=MESH)

    for way, shift in enumerate((1, -1)):

        @pl.when(jnp.logical_and(inward == -shift, jnp.logical_not(middle)))
        def _():
            tell(reach.at[way, 0], at_sub(on_chip(-shift, core)))

    for place, bit in enumerate(cell_bits):

        @pl.when((cell // bit) % 2 == 1)
        def _():
            tell(cell_reach.at[0, place], (partner(cell, bit), sub))

    def relay(distance):
        for way, shift in enumerate((1, -1)):

            @pl.when(jnp.logical_and(has_chip(-shift), has_chip(shift * (distance - 1))))
            def _():
                tell(reach.at[way, distance - 1], at_sub(on_chip(-shift, core)))

    def learn(distance):
        for way, shift in enumerate((1, -1)):

            known = has_chip(shift * distance)
            if distance == 1:
                known = jnp.logical_and(known, inward != shift)

            @pl.when(known)
            def _():
                pl.semaphore_wait(reach.at[way, distance - 1], 1)

    sends = []

    def rows_of(index):
        return pl.ds(pl.multiple_of(index * rows, rows), rows)

    def slots_of(index):
        return pl.ds(index * slots, slots)

    def heat_copy(source, target, device):
        return pltpu.make_async_remote_copy(
            src_ref=staged.at[slots_of(target)],
            dst_ref=slot_rise.at[:, rows_of(source)],
            send_sem=heat_send.at[target],
            recv_sem=heat_recv.at[source],
            device_id=at_sub(device),
            device_id_type=MESH,
        )

    def surf_copy(source, target, device):
        return pltpu.make_async_remote_copy(
            src_ref=conc.at[0, :, shells - 1, rows_of(target)],
            dst_ref=surface_rows.at[slots_of(source)],
            send_sem=surf_send.at[target],
            recv_sem=surf_recv.at[source],
            device_id=at_sub(device),
            device_id_type=MESH,
        )

    def curr_copy(source, target, device):
        return pltpu.make_async_remote_copy(
            src_ref=current.at[0, :, rows_of(target)],
            dst_ref=current_rows.at[slots_of(source)],
            send_sem=curr_send.at[target],
            recv_sem=curr_recv.at[source],
            device_id=at_sub(device),
            device_id_type=MESH,
        )

    inner = jnp.logical_and(has_chip(-1), has_chip(1))
    outer = jnp.logical_not(inner)

    def issue(distance, makers, when=True, within=None):
        for shift in (distance, -distance) if distance else (0,):

            wanted = jnp.logical_and(has_chip(shift), when)
            if distance and heat_copy not in makers:
                crossing = jnp.logical_and(chip + shift == theirs, distance > 0)
                wanted = jnp.logical_and(wanted, jnp.logical_not(crossing))
            if within is not None:
                wanted = jnp.logical_and(wanted, (inward == shift) == within)

            @pl.when(wanted)
            def _():
                for make in makers:
                    for place in range(PAIR) if distance else range(1, PAIR):
                        other = on_chip(shift, place if distance else (core + place) % PAIR)
                        make(sub, other, other).start()

    issue(1, (curr_copy, surf_copy), outer)
    for load in first_loads:
        load.wait()
    edges[0] = heat[0, :, 0]
    edges[1] = heat[0, :, rows - 1]
    start = jnp.int32(0)
    for index in range(subs):
        held = counts[index]
        for place in range(slots):
            layer = jnp.minimum(start + place, layers - 1)
            staged[index * slots + place] = heat[0, layer]
            slot_layer[index * slots + place] = layer
            border_out[index, place] = heat[0, layer, jnp.where(left, rows - 1, 0)]
        start = start + held
    faces[cell] = jnp.zeros((2, rows, gx), jnp.float32)

    issue(1, (heat_copy,), within=True)
    learn(1)
    if chips > 2:
        relay(2)
    issue(1, (heat_copy,), within=False)
    issue(0, (heat_copy, surf_copy, curr_copy))
    to_below = pltpu.make_async_remote_copy(
        src_ref=edges.at[0],
        dst_ref=high_edge,
        send_sem=edge_send.at[0],
        recv_sem=edge_recv.at[0],
        device_id=at_sub(jnp.maximum(sub - 1, 0)),
        device_id_type=MESH,
    )
    to_above = pltpu.make_async_remote_copy(
        src_ref=edges.at[1],
        dst_ref=low_edge,
        send_sem=edge_send.at[1],
        recv_sem=edge_recv.at[1],
        device_id=at_sub(jnp.minimum(sub + 1, subs - 1)),
        device_id_type=MESH,
    )

    @pl.when(sub > 0)
    def _():
        to_below.start()

    @pl.when(sub < subs - 1)
    def _():
        to_above.start()

    far = range(chips - 1, 1, -1)
    for distance in range(2, chips):
        learn(distance)
        if distance + 1 < chips:
            relay(distance + 1)
    bordering = jnp.logical_and(
        chip == ours + jnp.where(left, -1, 1), core == jnp.where(left, PAIR - 1, 0)
    )

    def border_copy(target):
        return pltpu.make_async_remote_copy(
            src_ref=border_out.at[target],
            dst_ref=border_in,
            send_sem=border_send.at[target],
            recv_sem=border_recv.at[0],
            device_id=at_sub(target),
            device_id_type=MESH,
        )

    def borders(act):
        @pl.when(bordering)
        def _():
            for place in range(half):
                act(border_copy(jnp.where(left, half + place, place)))

    borders(lambda copy: copy.start())
    for distance in far:
        issue(distance, (heat_copy,))
    for distance in far:
        issue(distance, (surf_copy,), inner)
    for distance in far:
        issue(distance, (surf_copy,), outer)

    def face_copies(source, device):
        return [
            pltpu.make_async_remote_copy(
                src_ref=heat_hbm.at[0, layer],
                dst_ref=faces.at[source, place],
                send_sem=face_send.at[2 * device + place],
                recv_sem=face_recv.at[2 * source + place],
                device_id=(device, sub),
                device_id_type=MESH,
            )
            for place, layer in ((0, 0), (1, layers - 1))
        ]

    for place, bit in enumerate(cell_bits):

        @pl.when((cell // bit) % 2 == 0)
        def _():
            pl.semaphore_wait(cell_reach.at[0, place], 1)

    def spread(place):
        tell(cell_reach.at[1, place], (partner(cell, cell_bits[place]), sub))

    if len(cell_bits) > 1:
        spread(0)

    def send_faces():
        for place in range(len(cell_bits) - 1):
            pl.semaphore_wait(cell_reach.at[1, place], 1)
            if place + 1 < len(cell_bits) - 1:
                spread(place + 1)
        for offset in range(1, cells):
            for copy in face_copies(cell, partner(cell, offset)):
                copy.start()
                sends.append(copy)


    mine = [
        pltpu.make_async_copy(
            conc.at[0, :, shells - 1, rows_of(sub)], surface_rows.at[slots_of(sub)], own_sem.at[2]
        ),
        pltpu.make_async_copy(
            current.at[0, :, rows_of(sub)], current_rows.at[slots_of(sub)], own_sem.at[3]
        ),
    ]
    for copy in mine:
        copy.start()
    slot_rise[:, rows_of(sub)] = staged[slots_of(sub)]

    def slot_of(layer, carry):
        total = jnp.int32(0)
        slot = layer
        for index in range(subs):
            total = total + counts[index]
            slot = slot + jnp.where(total <= layer, slots - counts[index], 0)
        layer_slot[layer] = jnp.minimum(slot, subs * slots - 1)
        return carry

    lax.fori_loop(0, layers, slot_of, jnp.int32(0))

    live_count = counts[sub]
    live = lax.broadcasted_iota(jnp.int32, (slots, rows, gx), 0) < live_count
    volumes = [((r + 1) ** 3 - r**3) / (3.0 * shells**3) for r in range(shells)]
    weights = [DIFFUSION_STEP * ((r + 1) ** 2 / shells**2 * shells) for r in range(shells - 1)]

    def particle(where):
        rise = slot_rise[:, where]
        speedup = jnp.exp(
            (DIFFUSION_ACTIVATION / BASE_KELVIN) * rise / (BASE_KELVIN + rise)
        )
        uppers = []
        values = []
        link = None
        for r in range(shells):
            right = volumes[r] * conc_in[:, r, where]
            if r == shells - 1:
                right = right - SURFACE_STEP * current_in[:, where]
            pivot = volumes[r]
            if r > 0:
                pivot = pivot + link * (1.0 - uppers[r - 1])
                right = right + link * values[r - 1]
            if r < shells - 1:
                next_link = weights[r] * speedup
                pivot = pivot + next_link
            inverse = 1.0 / pivot
            if r < shells - 1:
                uppers.append(next_link * inverse)
                link = next_link
            values.append(right * inverse)
        result = values[shells - 1]
        conc_in[:, shells - 1, where] = jnp.where(live, result, 0.0)
        for r in range(shells - 2, -1, -1):
            result = values[r] + uppers[r] * result
            conc_in[:, r, where] = jnp.where(live, result, 0.0)

    for load in loads:
        load.wait()
    near = [0] + arrivals[: 2 * PAIR - 1]
    rest = arrivals[2 * PAIR - 1 :]
    for count, offset in enumerate(near):
        other = partner(sub, offset)
        if offset:
            heat_copy(other, sub, other).wait_recv()
        particle(rows_of(other))
        if count == 0:
            send_faces()
        if count == 1:
            issue(1, (surf_copy, curr_copy), inner)
    row_index = lax.broadcasted_iota(jnp.int32, (rows, gx), 0)
    lane_index = lax.broadcasted_iota(jnp.int32, (rows, gx), 1)

    def smoothed(here, before, after):
        up = jnp.where(row_index == 0, before, pltpu.roll(here, 1, 0))
        down = jnp.where(row_index == rows - 1, after, pltpu.roll(here, rows - 1, 0))
        left_side = jnp.where(lane_index == 0, here, pltpu.roll(here, 1, 1))
        right_side = jnp.where(lane_index == gx - 1, here, pltpu.roll(here, gx - 1, 1))
        return here + INPLANE_CONDUCT * (down + up + right_side + left_side - 4.0 * here)

    def twin_copy(source, place):
        return pltpu.make_async_remote_copy(
            src_ref=twin_out.at[place],
            dst_ref=twin_in.at[:, slots_of(source % half)],
            send_sem=twin_send.at[place],
            recv_sem=twin_recv.at[source % half],
            device_id=at_sub(ours * PAIR + place),
            device_id_type=MESH,
        )

    def heat_from(chip_index):
        for place in range(PAIR):
            other = chip_index * PAIR + place
            heat_copy(other, sub, other).wait_recv()

    heat_from(theirs)
    border_copy(sub).wait_recv()
    for count in range(PAIR):
        place = jnp.where(left, count, PAIR - 1 - count)
        index = theirs * PAIR + place
        here = slot_rise[:, rows_of(index)]
        source, slope = kinetics(
            conc_in[:, shells - 1, rows_of(index)], here, current_in[:, rows_of(index)]
        )
        extra_here = source - slope * here
        for s in range(slots):
            first, last = index * rows, index * rows + rows - 1
            open_low = jnp.logical_and(jnp.logical_not(left), place == 0)
            open_high = jnp.logical_and(left, place == PAIR - 1)
            before = slot_rise[s, pl.ds(jnp.where(open_low, first, first - 1), 1)]
            after = slot_rise[s, pl.ds(jnp.where(open_high, last, last + 1), 1)]
            rim = border_in[pl.ds(s, 1)]
            before = jnp.where(open_low, rim, before)
            after = jnp.where(open_high, rim, after)
            twin_out[place, 0, s] = smoothed(here[s], before, after) + extra_here[s]
        twin_out[place, 1] = 1.0 - slope
        mine_too = sub == ours * PAIR + place

        @pl.when(mine_too)
        def _():
            twin_in[:, slots_of(sub % half)] = twin_out[place]

        @pl.when(jnp.logical_not(mine_too))
        def _():
            twin_copy(sub, place).start()

    for distance in far:
        issue(distance, (curr_copy,), inner)
    for distance in far:
        issue(distance, (curr_copy,), outer)

    @pl.when(sub > 0)
    def _():
        to_above.wait_recv()

    @pl.when(sub == 0)
    def _():
        low_edge[...] = edges[0]

    @pl.when(sub < subs - 1)
    def _():
        to_below.wait_recv()

    @pl.when(sub == subs - 1)
    def _():
        high_edge[...] = edges[1]

    for offset in range(1, cells):
        other = partner(cell, offset)
        for copy in face_copies(other, other):
            copy.wait_recv()

    def fill(layer, carry):
        base[layer] = smoothed(heat[0, layer], low_edge[pl.ds(layer, 1)], high_edge[pl.ds(layer, 1)])
        return carry

    lax.fori_loop(0, layers, fill, jnp.int32(0), unroll=2)
    lower_cell = contacts[0, cell]
    upper_cell = contacts[1, cell]
    below_face = jnp.where(lower_cell >= 0, faces[jnp.maximum(lower_cell, 0), 1], 0.0)
    above_face = jnp.where(upper_cell >= 0, faces[jnp.maximum(upper_cell, 0), 0], 0.0)
    share = CONTACT_CONDUCT / THROUGH_CONDUCT
    low_start = share * (below_face - heat[0, 0])
    high_start = share * (above_face - heat[0, layers - 1])
    own_start = jnp.where(left, low_start, high_start)
    other_start = jnp.where(left, high_start, low_start)

    def pair_copy(index, source, target):
        return pltpu.make_async_remote_copy(
            src_ref=source,
            dst_ref=target,
            send_sem=pair_send.at[index],
            recv_sem=pair_recv.at[index],
            device_id=at_sub(twin),
            device_id_type=MESH,
        )

    contact_copy = pair_copy(0, contact_out, contact_in)
    match_copy = pair_copy(1, match_out, match_in)
    part_copy = pair_copy(2, part, solved.at[pl.ds(own_first, own_slots)])

    @pl.when(middle)
    def _():
        contact_out[...] = other_start
        contact_copy.start()

    def prepare(offset):
        other = partner(sub, offset)
        if offset:
            surf_copy(other, sub, other).wait_recv()
            curr_copy(other, sub, other).wait_recv()
        else:
            for copy in mine:
                copy.wait()
        at = slots_of(other)
        rise = staged[at]
        source, slope = kinetics(surface_rows[at], rise, current_rows[at])
        extra[at] = source - slope * rise
        diagonal[at] = 1.0 - slope

    def eliminate(bank, low, fetch, start):
        pivot = jnp.full((rows, gx), 1.0, jnp.float32)
        before = jnp.full((rows, gx), 0.5, jnp.float32)
        total = start
        for step in range(own_slots):
            index = jnp.where(low, step, own_slots - 1 - step)
            owner = jnp.where(low, step // slots, subs - 1 - step // slots)
            filled = jnp.where(low, step % slots, slots - 1 - step % slots) < counts[owner]
            right, own = fetch(index)
            own = own + 2.0 * THROUGH_CONDUCT
            next_pivot = own * pivot - THROUGH_CONDUCT**2 * before
            next_total = right * pivot + THROUGH_CONDUCT * total
            inverse = 1.0 / next_pivot
            factors[bank, step] = jnp.where(filled, THROUGH_CONDUCT * pivot * inverse, 1.0)
            values[bank, step] = jnp.where(filled, next_total * inverse, 0.0)
            before = jnp.where(filled, pivot, before)
            pivot = jnp.where(filled, next_pivot, pivot)
            total = jnp.where(filled, next_total, total)
        inverse = 1.0 / pivot
        return THROUGH_CONDUCT * before * inverse, total * inverse

    def unwind(bank, low, result, target, first):
        for step in range(own_slots - 1, -1, -1):
            result = values[bank, step] + factors[bank, step] * result
            target[first + jnp.where(low, step, own_slots - 1 - step)] = result

    def from_rows(first):
        def fetch(index):
            slot = first + index
            return base[slot_layer[slot]] + extra[slot], diagonal[slot]

        return fetch

    def meeting(factor, value, other_factor, other_value):
        return (other_value + other_factor * value) / (1.0 - factor * other_factor)

    for offset in [0] + arrivals:
        if offset < half:
            prepare(offset)
    own_factor, own_value = eliminate(0, left, from_rows(own_first), own_start)

    @pl.when(middle)
    def _():
        match_out[0] = own_factor
        match_out[1] = own_value
        match_copy.start()
        for place in range(half):
            source = jnp.where(left, place, half + place)

            @pl.when(source != sub)
            def _():
                twin_copy(source, 0).wait_recv()

        contact_copy.wait_recv()
        factor, value = eliminate(
            1, left, lambda index: (twin_in[0, index], twin_in[1, index]), contact_in[...]
        )
        match_copy.wait_recv()
        unwind(1, left, meeting(factor, value, match_in[0], match_in[1]), part, 0)
        part_copy.start()

    for offset in rest:
        other = partner(sub, offset)

        @pl.when(other // PAIR != theirs)
        def _():
            heat_copy(other, sub, other).wait_recv()

        particle(rows_of(other))

    @pl.when(middle)
    def _():
        part_copy.wait_recv()
        rim = solved[jnp.where(left, own_slots, own_slots - slots)]
        for place in range(1, slots):
            beyond = solved[jnp.where(left, own_slots, own_slots - slots + place)]
            rim = jnp.where(counts[half - 1] > place, beyond, rim)
        unwind(0, left, rim, solved, own_first)
        contact_copy.wait_send()
        match_copy.wait_send()
        part_copy.wait_send()

    @pl.when(jnp.logical_not(middle))
    def _():
        for offset in arrivals:
            if offset >= half:
                prepare(offset)
        right = jnp.logical_not(left)
        factor, value = eliminate(1, right, from_rows(other_first), other_start)
        across = meeting(own_factor, own_value, factor, value)
        unwind(0, left, across, solved, own_first)
        back = meeting(factor, value, own_factor, own_value)
        unwind(1, right, back, solved, other_first)

    borders(lambda copy: copy.wait_send())
    for layer in range(layers):
        answer[0, layer] = solved[layer_slot[layer]]

    for place in range(PAIR):

        @pl.when(sub != ours * PAIR + place)
        def _():
            twin_copy(sub, place).wait_send()

    for offset in offsets:
        other = partner(sub, offset)
        heat_copy(sub, other, other).wait_send()

        @pl.when(jnp.logical_or(other // PAIR != theirs, offset < half))
        def _():
            surf_copy(sub, other, other).wait_send()
            curr_copy(sub, other, other).wait_send()

    for copy in sends:
        copy.wait_send()

    @pl.when(sub > 0)
    def _():
        to_below.wait_send()

    @pl.when(sub < subs - 1)
    def _():
        to_above.wait_send()


def finish(conc, answer, conc_new, heat_new, sem):
    slots = conc.shape[0]
    writes = [
        pltpu.make_async_copy(conc.at[s], conc_new.at[0, s], sem.at[s]) for s in range(slots)
    ]
    writes.append(pltpu.make_async_copy(answer, heat_new, sem.at[slots]))
    for write in writes:
        write.start()
    for write in writes:
        write.wait()


def per_device(cells, subs, shell_conc, heat_rise, layer_current, layer_counts, contacts):
    _, slots, shells, gy, gx = shell_conc.shape
    _, layers, rows, _ = heat_rise.shape
    f32 = jnp.float32
    dma = pltpu.SemaphoreType.DMA
    table = (layers, rows, gx)
    own_slots = subs // 2 * slots
    held = [
        pltpu.with_memory_space_constraint(array, pltpu.HBM)
        for array in (layer_counts, contacts.T, heat_rise, shell_conc, layer_current)
    ]
    conc, answer = pl.pallas_call(
        functools.partial(kernel, cells, subs),
        out_shape=(
            pltpu.VMEM((slots, shells, gy, gx), f32),
            pltpu.VMEM(heat_rise.shape, f32),
        ),
        in_specs=[
            pl.BlockSpec(memory_space=pltpu.HBM)
        ] * 5,
        out_specs=(pl.BlockSpec(memory_space=pltpu.VMEM),) * 2,
        scratch_shapes=[
            pltpu.VMEM(heat_rise.shape, f32),
            pltpu.VMEM((subs * slots, rows, gx), f32),
            pltpu.VMEM((slots, gy, gx), f32),
            pltpu.VMEM((slots, gy, gx), f32),
            pltpu.VMEM((subs * slots, rows, gx), f32),
            pltpu.VMEM((subs * slots, rows, gx), f32),
            pltpu.VMEM((2, layers, gx), f32),
            pltpu.VMEM((layers, gx), f32),
            pltpu.VMEM((layers, gx), f32),
            pltpu.VMEM((cells, 2, rows, gx), f32),
            pltpu.VMEM(table, f32),
            pltpu.VMEM((subs * slots, rows, gx), f32),
            pltpu.VMEM((subs * slots, rows, gx), f32),
            pltpu.SMEM((layers,), jnp.int32),
            pltpu.SMEM((subs * slots,), jnp.int32),
            pltpu.SMEM(layer_counts.shape, jnp.int32),
            pltpu.SMEM(contacts.shape[::-1], jnp.int32),
            pltpu.VMEM((PAIR, 2, slots, rows, gx), f32),
            pltpu.VMEM((2, own_slots, rows, gx), f32),
            pltpu.VMEM((subs * slots, rows, gx), f32),
            pltpu.VMEM((2, own_slots, rows, gx), f32),
            pltpu.VMEM((2, own_slots, rows, gx), f32),
            pltpu.VMEM((rows, gx), f32),
            pltpu.VMEM((rows, gx), f32),
            pltpu.VMEM((2, rows, gx), f32),
            pltpu.VMEM((2, rows, gx), f32),
            pltpu.VMEM((own_slots, rows, gx), f32),
            pltpu.VMEM((subs, slots, gx), f32),
            pltpu.VMEM((slots, gx), f32),
            pltpu.SemaphoreType.REGULAR((2, max(subs // PAIR, 2))),
            pltpu.SemaphoreType.REGULAR((2, max(cells.bit_length() - 1, 1))),
            dma((7,)),
            dma((subs,)),
            dma((subs,)),
            dma((subs,)),
            dma((subs,)),
            dma((subs,)),
            dma((subs,)),
            dma((2,)),
            dma((2,)),
            dma((2 * cells,)),
            dma((2 * cells,)),
            dma((PAIR,)),
            dma((subs // 2,)),
            dma((3,)),
            dma((3,)),
            dma((subs,)),
            dma((1,)),
        ],
        compiler_params=pltpu.CompilerParams(
            collective_id=0, has_side_effects=True, vmem_limit_bytes=GRANT
        ),
    )(*held)
    conc_new, heat_new = pl.pallas_call(
        finish,
        out_shape=(
            jax.ShapeDtypeStruct(shell_conc.shape, f32),
            jax.ShapeDtypeStruct(heat_rise.shape, f32),
        ),
        in_specs=[pl.BlockSpec(memory_space=pltpu.VMEM)] * 2,
        out_specs=(
            pl.BlockSpec(memory_space=pl.ANY),
            pl.BlockSpec(memory_space=pl.ANY),
        ),
        scratch_shapes=[dma((slots + 1,))],
        compiler_params=pltpu.CompilerParams(vmem_limit_bytes=GRANT),
    )(conc, answer)
    return conc_new, heat_new


def solution(mesh):
    in_specs = (
        P("cell", "sub", None, None, None),
        P("cell", None, "sub", None),
        P("cell", "sub", None, None),
        P(),
        P(),
    )
    out_specs = (P("cell", "sub", None, None, None), P("cell", None, "sub", None))
    body = functools.partial(per_device, mesh.shape["cell"], mesh.shape["sub"])
    return jax.shard_map(
        body, mesh=mesh, in_specs=in_specs, out_specs=out_specs, check_vma=False
    )
```

```python
import functools

import jax
import jax.numpy as jnp
from jax import lax
from jax.experimental import pallas as pl
from jax.experimental.pallas import tpu as pltpu
from jax.sharding import PartitionSpec as P

BASE_KELVIN = 298.15
RATE_ACTIVATION = 5000.0
DIFFUSION_ACTIVATION = 3000.0
RATE_CONSTANT = 0.5
VOLT_PER_KELVIN = 2.0 * 8.314462618 / 96485.33212
HEAT_SCALE = 10.0
ENTROPY_SLOPE = 0.001
DIFFUSION_STEP = 0.005
SURFACE_STEP = 0.005
INPLANE_CONDUCT = 0.25
THROUGH_CONDUCT = 2.0
CONTACT_CONDUCT = 0.5
MESH = pl.DeviceIdType.MESH
GRANT = 24 << 20
PAIR = 2


def partner(me, offset):
    bit = 1
    result = me
    while bit <= offset:
        if offset & bit:
            result = result + bit * (1 - 2 * ((me // bit) % 2))
        bit *= 2
    return result


def inverse_sine(value):
    magnitude = jnp.abs(value)
    rooted = jnp.sqrt(1.0 + magnitude * magnitude)
    positive = jnp.log1p(magnitude + magnitude * magnitude / (1.0 + rooted))
    return jnp.where(value < 0.0, -positive, positive), rooted


def kinetics(surface, rise, current):
    kelvin = BASE_KELVIN + rise
    per_kelvin = 1.0 / kelvin
    reciprocal = rise * (1.0 / BASE_KELVIN) * per_kelvin
    ratio_rate = (
        current
        * jnp.exp(-RATE_ACTIVATION * reciprocal)
        * lax.rsqrt(surface * (1.0 - surface))
        * (0.5 / RATE_CONSTANT)
    )
    arcsine, rooted = inverse_sine(ratio_rate)
    entropic = ENTROPY_SLOPE * (0.5 - surface)
    scaled = HEAT_SCALE * current
    common = VOLT_PER_KELVIN * arcsine + entropic
    source = scaled * kelvin * common
    heat_slope = scaled * (
        common - (VOLT_PER_KELVIN * RATE_ACTIVATION) * ratio_rate * per_kelvin / rooted
    )
    return source, heat_slope


def kernel(
    cells, subs,
    counts_hbm, contacts_hbm, heat_hbm, conc, current,
    conc_in, answer,
    heat, staged, slot_rise, current_in, surface_rows, current_rows,
    edges, low_edge, high_edge, faces, base, extra, diagonal, layer_slot, slot_layer, counts, contacts,
    twin_out, twin_in, solved, factors, values, contact_out, contact_in, match_out, match_in, part, border_out, border_in,
    reach, cell_reach, own_sem, heat_send, heat_recv, surf_send, surf_recv, curr_send, curr_recv,
    edge_send, edge_recv, face_send, face_recv,
    twin_send, twin_recv, pair_send, pair_recv, border_send, border_recv,
):
    cell = lax.axis_index("cell")
    sub = lax.axis_index("sub")
    slots, shells, gy, gx = conc_in.shape
    layers, rows, _ = heat.shape[1:]

    offsets = list(range(1, subs))
    arrivals = offsets[: PAIR - 1] + offsets[2 * PAIR - 2 : PAIR - 2 : -1] + offsets[: 2 * PAIR - 2 : -1]
    chip, core, chips = sub // PAIR, sub % PAIR, subs // PAIR
    cell_bits = [1 << bit for bit in range(cells.bit_length() - 1)]

    half = subs // 2
    own_slots = half * slots
    left = 2 * chip < chips
    ours = jnp.where(left, chips // 2 - 1, chips // 2)
    theirs = chips - 1 - ours
    own_first = jnp.where(left, 0, own_slots)
    other_first = own_slots - own_first
    twin = theirs * PAIR + core

    def has_chip(shift):
        return jnp.logical_and(chip + shift >= 0, chip + shift < chips)

    def on_chip(shift, place):
        return jnp.clip(chip + shift, 0, chips - 1) * PAIR + place

    def at_sub(index):
        return (cell, index)

    first_loads = [
        pltpu.make_async_copy(counts_hbm, counts, own_sem.at[5]),
        pltpu.make_async_copy(heat_hbm, heat, own_sem.at[4]),
        pltpu.make_async_copy(contacts_hbm, contacts, own_sem.at[6]),
    ]
    for load in first_loads:
        load.start()
    barrier = pltpu.get_barrier_semaphore()

    def greet(device):
        pl.semaphore_signal(barrier, inc=1, device_id=device, device_id_type=MESH)

    for place in range(1, PAIR):
        greet(at_sub(chip * PAIR + (core + place) % PAIR))
    inward = jnp.where(2 * chip < chips, 1, -1)
    middle = jnp.logical_or(chip == chips // 2 - 1, chip == chips // 2)
    for shift in (-1, 1):

        @pl.when(jnp.logical_and(has_chip(shift), jnp.logical_or(inward != shift, middle)))
        def _():
            for place in range(PAIR):
                greet(at_sub(on_chip(shift, place)))

    for bit in cell_bits:

        @pl.when((cell // bit) % 2 == 0)
        def _():
            greet((partner(cell, bit), sub))

    loads = [
        pltpu.make_async_copy(current.at[0], current_in, own_sem.at[0]),
        pltpu.make_async_copy(conc.at[0], conc_in, own_sem.at[1]),
    ]
    for load in loads:
        load.start()

    lower = sum((cell // bit) % 2 for bit in cell_bits)
    pl.semaphore_wait(barrier, PAIR - 1 + (PAIR if chips > 1 else 0) + lower)

    def tell(semaphore, device):
        pl.semaphore_signal(semaphore, inc=1, device_id=device, device_id_type=MESH)

    for way, shift in enumerate((1, -1)):

        @pl.when(jnp.logical_and(inward == -shift, jnp.logical_not(middle)))
        def _():
            tell(reach.at[way, 0], at_sub(on_chip(-shift, core)))

    for place, bit in enumerate(cell_bits):

        @pl.when((cell // bit) % 2 == 1)
        def _():
            tell(cell_reach.at[0, place], (partner(cell, bit), sub))

    def relay(distance):
        for way, shift in enumerate((1, -1)):

            @pl.when(jnp.logical_and(has_chip(-shift), has_chip(shift * (distance - 1))))
            def _():
                tell(reach.at[way, distance - 1], at_sub(on_chip(-shift, core)))

    def learn(distance):
        for way, shift in enumerate((1, -1)):

            known = has_chip(shift * distance)
            if distance == 1:
                known = jnp.logical_and(known, inward != shift)

            @pl.when(known)
            def _():
                pl.semaphore_wait(reach.at[way, distance - 1], 1)

    sends = []

    def rows_of(index):
        return pl.ds(pl.multiple_of(index * rows, rows), rows)

    def slots_of(index):
        return pl.ds(index * slots, slots)

    def heat_copy(source, target, device):
        return pltpu.make_async_remote_copy(
            src_ref=staged.at[slots_of(target)],
            dst_ref=slot_rise.at[:, rows_of(source)],
            send_sem=heat_send.at[target],
            recv_sem=heat_recv.at[source],
            device_id=at_sub(device),
            device_id_type=MESH,
        )

    def surf_copy(source, target, device):
        return pltpu.make_async_remote_copy(
            src_ref=conc.at[0, :, shells - 1, rows_of(target)],
            dst_ref=surface_rows.at[slots_of(source)],
            send_sem=surf_send.at[target],
            recv_sem=surf_recv.at[source],
            device_id=at_sub(device),
            device_id_type=MESH,
        )

    def curr_copy(source, target, device):
        return pltpu.make_async_remote_copy(
            src_ref=current.at[0, :, rows_of(target)],
            dst_ref=current_rows.at[slots_of(source)],
            send_sem=curr_send.at[target],
            recv_sem=curr_recv.at[source],
            device_id=at_sub(device),
            device_id_type=MESH,
        )

    inner = jnp.logical_and(has_chip(-1), has_chip(1))
    outer = jnp.logical_not(inner)

    def issue(distance, makers, when=True, within=None):
        for shift in (distance, -distance) if distance else (0,):

            wanted = jnp.logical_and(has_chip(shift), when)
            if distance and heat_copy not in makers:
                crossing = jnp.logical_and(chip + shift == theirs, distance > 0)
                wanted = jnp.logical_and(wanted, jnp.logical_not(crossing))
            if within is not None:
                wanted = jnp.logical_and(wanted, (inward == shift) == within)

            @pl.when(wanted)
            def _():
                for make in makers:
                    for place in range(PAIR) if distance else range(1, PAIR):
                        other = on_chip(shift, place if distance else (core + place) % PAIR)
                        make(sub, other, other).start()

    issue(1, (curr_copy,), outer)
    for load in first_loads:
        load.wait()
    edges[0] = heat[0, :, 0]
    edges[1] = heat[0, :, rows - 1]
    start = jnp.int32(0)
    for index in range(subs):
        held = counts[index]
        for place in range(slots):
            layer = jnp.minimum(start + place, layers - 1)
            staged[index * slots + place] = heat[0, layer]
            slot_layer[index * slots + place] = layer
            border_out[index, place] = heat[0, layer, jnp.where(left, rows - 1, 0)]
        start = start + held
    faces[cell] = jnp.zeros((2, rows, gx), jnp.float32)

    issue(1, (heat_copy,), within=True)
    learn(1)
    if chips > 2:
        relay(2)
    issue(1, (heat_copy,), within=False)
    issue(1, (surf_copy,), outer)
    issue(0, (heat_copy, surf_copy, curr_copy))
    to_below = pltpu.make_async_remote_copy(
        src_ref=edges.at[0],
        dst_ref=high_edge,
        send_sem=edge_send.at[0],
        recv_sem=edge_recv.at[0],
        device_id=at_sub(jnp.maximum(sub - 1, 0)),
        device_id_type=MESH,
    )
    to_above = pltpu.make_async_remote_copy(
        src_ref=edges.at[1],
        dst_ref=low_edge,
        send_sem=edge_send.at[1],
        recv_sem=edge_recv.at[1],
        device_id=at_sub(jnp.minimum(sub + 1, subs - 1)),
        device_id_type=MESH,
    )

    @pl.when(sub > 0)
    def _():
        to_below.start()

    @pl.when(sub < subs - 1)
    def _():
        to_above.start()

    far = range(chips - 1, 1, -1)
    for distance in range(2, chips):
        learn(distance)
        if distance + 1 < chips:
            relay(distance + 1)
    bordering = jnp.logical_and(
        chip == ours + jnp.where(left, -1, 1), core == jnp.where(left, PAIR - 1, 0)
    )

    def border_copy(target):
        return pltpu.make_async_remote_copy(
            src_ref=border_out.at[target],
            dst_ref=border_in,
            send_sem=border_send.at[target],
            recv_sem=border_recv.at[0],
            device_id=at_sub(target),
            device_id_type=MESH,
        )

    def borders(act):
        @pl.when(bordering)
        def _():
            for place in range(half):
                act(border_copy(jnp.where(left, half + place, place)))

    borders(lambda copy: copy.start())
    for distance in far:
        issue(distance, (heat_copy,))
    for distance in far:
        issue(distance, (surf_copy,), inner)
    for distance in far:
        issue(distance, (surf_copy,), outer)

    def face_copies(source, device):
        return [
            pltpu.make_async_remote_copy(
                src_ref=heat_hbm.at[0, layer],
                dst_ref=faces.at[source, place],
                send_sem=face_send.at[2 * device + place],
                recv_sem=face_recv.at[2 * source + place],
                device_id=(device, sub),
                device_id_type=MESH,
            )
            for place, layer in ((0, 0), (1, layers - 1))
        ]

    for place, bit in enumerate(cell_bits):

        @pl.when((cell // bit) % 2 == 0)
        def _():
            pl.semaphore_wait(cell_reach.at[0, place], 1)

    def spread(place):
        tell(cell_reach.at[1, place], (partner(cell, cell_bits[place]), sub))

    if len(cell_bits) > 1:
        spread(0)

    def send_faces():
        for place in range(len(cell_bits) - 1):
            pl.semaphore_wait(cell_reach.at[1, place], 1)
            if place + 1 < len(cell_bits) - 1:
                spread(place + 1)
        for offset in range(1, cells):
            for copy in face_copies(cell, partner(cell, offset)):
                copy.start()
                sends.append(copy)


    mine = [
        pltpu.make_async_copy(
            conc.at[0, :, shells - 1, rows_of(sub)], surface_rows.at[slots_of(sub)], own_sem.at[2]
        ),
        pltpu.make_async_copy(
            current.at[0, :, rows_of(sub)], current_rows.at[slots_of(sub)], own_sem.at[3]
        ),
    ]
    for copy in mine:
        copy.start()
    slot_rise[:, rows_of(sub)] = staged[slots_of(sub)]

    def slot_of(layer, carry):
        total = jnp.int32(0)
        slot = layer
        for index in range(subs):
            total = total + counts[index]
            slot = slot + jnp.where(total <= layer, slots - counts[index], 0)
        layer_slot[layer] = jnp.minimum(slot, subs * slots - 1)
        return carry

    lax.fori_loop(0, layers, slot_of, jnp.int32(0))

    live_count = counts[sub]
    live = lax.broadcasted_iota(jnp.int32, (slots, rows, gx), 0) < live_count
    volumes = [((r + 1) ** 3 - r**3) / (3.0 * shells**3) for r in range(shells)]
    weights = [DIFFUSION_STEP * ((r + 1) ** 2 / shells**2 * shells) for r in range(shells - 1)]

    def particle(where):
        rise = slot_rise[:, where]
        speedup = jnp.exp(
            (DIFFUSION_ACTIVATION / BASE_KELVIN) * rise / (BASE_KELVIN + rise)
        )
        uppers = []
        values = []
        link = None
        for r in range(shells):
            right = volumes[r] * conc_in[:, r, where]
            if r == shells - 1:
                right = right - SURFACE_STEP * current_in[:, where]
            pivot = volumes[r]
            if r > 0:
                pivot = pivot + link * (1.0 - uppers[r - 1])
                right = right + link * values[r - 1]
            if r < shells - 1:
                next_link = weights[r] * speedup
                pivot = pivot + next_link
            inverse = 1.0 / pivot
            if r < shells - 1:
                uppers.append(next_link * inverse)
                link = next_link
            values.append(right * inverse)
        result = values[shells - 1]
        conc_in[:, shells - 1, where] = jnp.where(live, result, 0.0)
        for r in range(shells - 2, -1, -1):
            result = values[r] + uppers[r] * result
            conc_in[:, r, where] = jnp.where(live, result, 0.0)

    for load in loads:
        load.wait()
    near = [0] + arrivals[: 2 * PAIR - 1]
    rest = arrivals[2 * PAIR - 1 :]
    for count, offset in enumerate(near):
        other = partner(sub, offset)
        if offset:
            heat_copy(other, sub, other).wait_recv()
        particle(rows_of(other))
        if count == 0:
            send_faces()
        if count == 1:
            issue(1, (surf_copy, curr_copy), inner)
    row_index = lax.broadcasted_iota(jnp.int32, (rows, gx), 0)
    lane_index = lax.broadcasted_iota(jnp.int32, (rows, gx), 1)

    def smoothed(here, before, after):
        up = jnp.where(row_index == 0, before, pltpu.roll(here, 1, 0))
        down = jnp.where(row_index == rows - 1, after, pltpu.roll(here, rows - 1, 0))
        left_side = jnp.where(lane_index == 0, here, pltpu.roll(here, 1, 1))
        right_side = jnp.where(lane_index == gx - 1, here, pltpu.roll(here, gx - 1, 1))
        return here + INPLANE_CONDUCT * (down + up + right_side + left_side - 4.0 * here)

    def twin_copy(source, place):
        return pltpu.make_async_remote_copy(
            src_ref=twin_out.at[place],
            dst_ref=twin_in.at[:, slots_of(source % half)],
            send_sem=twin_send.at[place],
            recv_sem=twin_recv.at[source % half],
            device_id=at_sub(ours * PAIR + place),
            device_id_type=MESH,
        )

    def heat_from(chip_index):
        for place in range(PAIR):
            other = chip_index * PAIR + place
            heat_copy(other, sub, other).wait_recv()

    heat_from(theirs)
    border_copy(sub).wait_recv()
    for count in range(PAIR):
        place = jnp.where(left, count, PAIR - 1 - count)
        index = theirs * PAIR + place
        here = slot_rise[:, rows_of(index)]
        source, slope = kinetics(
            conc_in[:, shells - 1, rows_of(index)], here, current_in[:, rows_of(index)]
        )
        extra_here = source - slope * here
        for s in range(slots):
            first, last = index * rows, index * rows + rows - 1
            open_low = jnp.logical_and(jnp.logical_not(left), place == 0)
            open_high = jnp.logical_and(left, place == PAIR - 1)
            before = slot_rise[s, pl.ds(jnp.where(open_low, first, first - 1), 1)]
            after = slot_rise[s, pl.ds(jnp.where(open_high, last, last + 1), 1)]
            rim = border_in[pl.ds(s, 1)]
            before = jnp.where(open_low, rim, before)
            after = jnp.where(open_high, rim, after)
            twin_out[place, 0, s] = smoothed(here[s], before, after) + extra_here[s]
        twin_out[place, 1] = 1.0 - slope
        mine_too = sub == ours * PAIR + place

        @pl.when(mine_too)
        def _():
            twin_in[:, slots_of(sub % half)] = twin_out[place]

        @pl.when(jnp.logical_not(mine_too))
        def _():
            twin_copy(sub, place).start()

    for distance in far:
        issue(distance, (curr_copy,), inner)
    for distance in far:
        issue(distance, (curr_copy,), outer)

    @pl.when(sub > 0)
    def _():
        to_above.wait_recv()

    @pl.when(sub == 0)
    def _():
        low_edge[...] = edges[0]

    @pl.when(sub < subs - 1)
    def _():
        to_below.wait_recv()

    @pl.when(sub == subs - 1)
    def _():
        high_edge[...] = edges[1]

    for offset in range(1, cells):
        other = partner(cell, offset)
        for copy in face_copies(other, other):
            copy.wait_recv()

    def fill(layer, carry):
        base[layer] = smoothed(heat[0, layer], low_edge[pl.ds(layer, 1)], high_edge[pl.ds(layer, 1)])
        return carry

    lax.fori_loop(0, layers, fill, jnp.int32(0), unroll=2)
    lower_cell = contacts[0, cell]
    upper_cell = contacts[1, cell]
    below_face = jnp.where(lower_cell >= 0, faces[jnp.maximum(lower_cell, 0), 1], 0.0)
    above_face = jnp.where(upper_cell >= 0, faces[jnp.maximum(upper_cell, 0), 0], 0.0)
    share = CONTACT_CONDUCT / THROUGH_CONDUCT
    low_start = share * (below_face - heat[0, 0])
    high_start = share * (above_face - heat[0, layers - 1])
    own_start = jnp.where(left, low_start, high_start)
    other_start = jnp.where(left, high_start, low_start)

    def pair_copy(index, source, target):
        return pltpu.make_async_remote_copy(
            src_ref=source,
            dst_ref=target,
            send_sem=pair_send.at[index],
            recv_sem=pair_recv.at[index],
            device_id=at_sub(twin),
            device_id_type=MESH,
        )

    contact_copy = pair_copy(0, contact_out, contact_in)
    match_copy = pair_copy(1, match_out, match_in)
    part_copy = pair_copy(2, part, solved.at[pl.ds(own_first, own_slots)])

    @pl.when(middle)
    def _():
        contact_out[...] = other_start
        contact_copy.start()

    def prepare(offset):
        other = partner(sub, offset)
        if offset:
            surf_copy(other, sub, other).wait_recv()
            curr_copy(other, sub, other).wait_recv()
        else:
            for copy in mine:
                copy.wait()
        at = slots_of(other)
        rise = staged[at]
        source, slope = kinetics(surface_rows[at], rise, current_rows[at])
        extra[at] = source - slope * rise
        diagonal[at] = 1.0 - slope

    def eliminate(bank, low, fetch, start):
        pivot = jnp.full((rows, gx), 1.0, jnp.float32)
        before = jnp.full((rows, gx), 0.5, jnp.float32)
        total = start
        for step in range(own_slots):
            index = jnp.where(low, step, own_slots - 1 - step)
            owner = jnp.where(low, step // slots, subs - 1 - step // slots)
            filled = jnp.where(low, step % slots, slots - 1 - step % slots) < counts[owner]
            right, own = fetch(index)
            own = own + 2.0 * THROUGH_CONDUCT
            next_pivot = own * pivot - THROUGH_CONDUCT**2 * before
            next_total = right * pivot + THROUGH_CONDUCT * total
            inverse = 1.0 / next_pivot
            factors[bank, step] = jnp.where(filled, THROUGH_CONDUCT * pivot * inverse, 1.0)
            values[bank, step] = jnp.where(filled, next_total * inverse, 0.0)
            before = jnp.where(filled, pivot, before)
            pivot = jnp.where(filled, next_pivot, pivot)
            total = jnp.where(filled, next_total, total)
        inverse = 1.0 / pivot
        return THROUGH_CONDUCT * before * inverse, total * inverse

    def unwind(bank, low, result, target, first):
        for step in range(own_slots - 1, -1, -1):
            result = values[bank, step] + factors[bank, step] * result
            target[first + jnp.where(low, step, own_slots - 1 - step)] = result

    def from_rows(first):
        def fetch(index):
            slot = first + index
            return base[slot_layer[slot]] + extra[slot], diagonal[slot]

        return fetch

    def meeting(factor, value, other_factor, other_value):
        return (other_value + other_factor * value) / (1.0 - factor * other_factor)

    for offset in [0] + arrivals:
        if offset < half:
            prepare(offset)
    own_factor, own_value = eliminate(0, left, from_rows(own_first), own_start)

    @pl.when(middle)
    def _():
        match_out[0] = own_factor
        match_out[1] = own_value
        match_copy.start()
        for place in range(half):
            source = jnp.where(left, place, half + place)

            @pl.when(source != sub)
            def _():
                twin_copy(source, 0).wait_recv()

        contact_copy.wait_recv()
        factor, value = eliminate(
            1, left, lambda index: (twin_in[0, index], twin_in[1, index]), contact_in[...]
        )
        match_copy.wait_recv()
        unwind(1, left, meeting(factor, value, match_in[0], match_in[1]), part, 0)
        part_copy.start()

    for offset in rest:
        other = partner(sub, offset)

        @pl.when(other // PAIR != theirs)
        def _():
            heat_copy(other, sub, other).wait_recv()

        particle(rows_of(other))

    @pl.when(middle)
    def _():
        part_copy.wait_recv()
        rim = solved[jnp.where(left, own_slots, own_slots - slots)]
        for place in range(1, slots):
            beyond = solved[jnp.where(left, own_slots, own_slots - slots + place)]
            rim = jnp.where(counts[half - 1] > place, beyond, rim)
        unwind(0, left, rim, solved, own_first)
        contact_copy.wait_send()
        match_copy.wait_send()
        part_copy.wait_send()

    @pl.when(jnp.logical_not(middle))
    def _():
        for offset in arrivals:
            if offset >= half:
                prepare(offset)
        right = jnp.logical_not(left)
        factor, value = eliminate(1, right, from_rows(other_first), other_start)
        across = meeting(own_factor, own_value, factor, value)
        unwind(0, left, across, solved, own_first)
        back = meeting(factor, value, own_factor, own_value)
        unwind(1, right, back, solved, other_first)

    borders(lambda copy: copy.wait_send())
    for layer in range(layers):
        answer[0, layer] = solved[layer_slot[layer]]

    for place in range(PAIR):

        @pl.when(sub != ours * PAIR + place)
        def _():
            twin_copy(sub, place).wait_send()

    for offset in offsets:
        other = partner(sub, offset)
        heat_copy(sub, other, other).wait_send()

        @pl.when(jnp.logical_or(other // PAIR != theirs, offset < half))
        def _():
            surf_copy(sub, other, other).wait_send()
            curr_copy(sub, other, other).wait_send()

    for copy in sends:
        copy.wait_send()

    @pl.when(sub > 0)
    def _():
        to_below.wait_send()

    @pl.when(sub < subs - 1)
    def _():
        to_above.wait_send()


def finish(conc, answer, conc_new, heat_new, sem):
    slots = conc.shape[0]
    writes = [
        pltpu.make_async_copy(conc.at[s], conc_new.at[0, s], sem.at[s]) for s in range(slots)
    ]
    writes.append(pltpu.make_async_copy(answer, heat_new, sem.at[slots]))
    for write in writes:
        write.start()
    for write in writes:
        write.wait()


def per_device(cells, subs, shell_conc, heat_rise, layer_current, layer_counts, contacts):
    _, slots, shells, gy, gx = shell_conc.shape
    _, layers, rows, _ = heat_rise.shape
    f32 = jnp.float32
    dma = pltpu.SemaphoreType.DMA
    table = (layers, rows, gx)
    own_slots = subs // 2 * slots
    held = [
        pltpu.with_memory_space_constraint(array, pltpu.HBM)
        for array in (layer_counts, contacts.T, heat_rise, shell_conc, layer_current)
    ]
    conc, answer = pl.pallas_call(
        functools.partial(kernel, cells, subs),
        out_shape=(
            pltpu.VMEM((slots, shells, gy, gx), f32),
            pltpu.VMEM(heat_rise.shape, f32),
        ),
        in_specs=[
            pl.BlockSpec(memory_space=pltpu.HBM)
        ] * 5,
        out_specs=(pl.BlockSpec(memory_space=pltpu.VMEM),) * 2,
        scratch_shapes=[
            pltpu.VMEM(heat_rise.shape, f32),
            pltpu.VMEM((subs * slots, rows, gx), f32),
            pltpu.VMEM((slots, gy, gx), f32),
            pltpu.VMEM((slots, gy, gx), f32),
            pltpu.VMEM((subs * slots, rows, gx), f32),
            pltpu.VMEM((subs * slots, rows, gx), f32),
            pltpu.VMEM((2, layers, gx), f32),
            pltpu.VMEM((layers, gx), f32),
            pltpu.VMEM((layers, gx), f32),
            pltpu.VMEM((cells, 2, rows, gx), f32),
            pltpu.VMEM(table, f32),
            pltpu.VMEM((subs * slots, rows, gx), f32),
            pltpu.VMEM((subs * slots, rows, gx), f32),
            pltpu.SMEM((layers,), jnp.int32),
            pltpu.SMEM((subs * slots,), jnp.int32),
            pltpu.SMEM(layer_counts.shape, jnp.int32),
            pltpu.SMEM(contacts.shape[::-1], jnp.int32),
            pltpu.VMEM((PAIR, 2, slots, rows, gx), f32),
            pltpu.VMEM((2, own_slots, rows, gx), f32),
            pltpu.VMEM((subs * slots, rows, gx), f32),
            pltpu.VMEM((2, own_slots, rows, gx), f32),
            pltpu.VMEM((2, own_slots, rows, gx), f32),
            pltpu.VMEM((rows, gx), f32),
            pltpu.VMEM((rows, gx), f32),
            pltpu.VMEM((2, rows, gx), f32),
            pltpu.VMEM((2, rows, gx), f32),
            pltpu.VMEM((own_slots, rows, gx), f32),
            pltpu.VMEM((subs, slots, gx), f32),
            pltpu.VMEM((slots, gx), f32),
            pltpu.SemaphoreType.REGULAR((2, max(subs // PAIR, 2))),
            pltpu.SemaphoreType.REGULAR((2, max(cells.bit_length() - 1, 1))),
            dma((7,)),
            dma((subs,)),
            dma((subs,)),
            dma((subs,)),
            dma((subs,)),
            dma((subs,)),
            dma((subs,)),
            dma((2,)),
            dma((2,)),
            dma((2 * cells,)),
            dma((2 * cells,)),
            dma((PAIR,)),
            dma((subs // 2,)),
            dma((3,)),
            dma((3,)),
            dma((subs,)),
            dma((1,)),
        ],
        compiler_params=pltpu.CompilerParams(
            collective_id=0, has_side_effects=True, vmem_limit_bytes=GRANT
        ),
    )(*held)
    conc_new, heat_new = pl.pallas_call(
        finish,
        out_shape=(
            jax.ShapeDtypeStruct(shell_conc.shape, f32),
            jax.ShapeDtypeStruct(heat_rise.shape, f32),
        ),
        in_specs=[pl.BlockSpec(memory_space=pltpu.VMEM)] * 2,
        out_specs=(
            pl.BlockSpec(memory_space=pl.ANY),
            pl.BlockSpec(memory_space=pl.ANY),
        ),
        scratch_shapes=[dma((slots + 1,))],
        compiler_params=pltpu.CompilerParams(vmem_limit_bytes=GRANT),
    )(conc, answer)
    return conc_new, heat_new


def solution(mesh):
    in_specs = (
        P("cell", "sub", None, None, None),
        P("cell", None, "sub", None),
        P("cell", "sub", None, None),
        P(),
        P(),
    )
    out_specs = (P("cell", "sub", None, None, None), P("cell", None, "sub", None))
    body = functools.partial(per_device, mesh.shape["cell"], mesh.shape["sub"])
    return jax.shard_map(
        body, mesh=mesh, in_specs=in_specs, out_specs=out_specs, check_vma=False
    )
```
